32 devices in a mesh: dp: 8 (over z, y), tensor: 4 (over x, core).
Axes of the slice: x: 2, y: 2, z: 4, core: 2. Of those that a mesh axis runs over, the one named last changes fastest.
Arguments:
- tokens: bfloat16 [4096, 768], P(('dp', 'tensor')), may hold values from -6 to 6
- chars: bfloat16 [16384, 256], P(('dp', 'tensor')), may hold values from -6 to 6
- lengths: int32 [8, 512], P('dp'), may hold values from 1 to 8, 2048 in all within a row
- mask: int32 [8, 512], P('dp'), may hold values 0 or 1
- qkv_weight: bfloat16 [768, 3, 12, 64], P(None, None, 'tensor'), may hold values from -0.21875 to 0.21875
- qkv_bias: float32 [2, 12, 64], P(None, 'tensor'), may hold values from -2 to 2
- out_weight: bfloat16 [12, 64, 768], P('tensor'), may hold values from -1.75 to 1.75
- out_bias: float32 [768], replicated, may hold values from -2 to 2
- attn_gain: float32 [768], replicated, may hold values from 0.5 to 1.5
- attn_shift: float32 [768], replicated, may hold values from -2 to 2
- ffn_in_weight: bfloat16 [768, 3072], P(None, 'tensor'), may hold values from -0.21875 to 0.21875
- ffn_in_bias: float32 [3072], P('tensor'), may hold values from -3 to 3
- ffn_out_weight: bfloat16 [3072, 768], P('tensor'), may hold values from -0.15625 to 0.15625
- ffn_out_bias: float32 [768], replicated, may hold values from -2 to 2
- ffn_gain: float32 [768], replicated, may hold values from 0.5 to 1.5
- ffn_shift: float32 [768], replicated, may hold values from -2 to 2
- gru_weight: bfloat16 [256, 2, 2, 384], P(None, None, None, 'tensor'), may hold values from -0.375 to 0.375
- gate_bias: float32 [2, 384], P(None, 'tensor'), may hold values from -6 to 0
- cand_bias: float32 [2, 384], P(None, 'tensor'), may hold values from -3 to 3
- char_weight: bfloat16 [2, 384, 768], P(None, 'tensor'), may hold values from -0.21875 to 0.21875
- char_bias: float32 [768], replicated, may hold values from -2 to 2
- merge_weight: bfloat16 [3, 1536, 1536], P(None, None, 'tensor'), may hold values from -0.09375 to 0.09375
- merge_bias: float32 [1536], P('tensor'), may hold values from -2 to 2
- token_gain: float32 [768], replicated, may hold values from 0.5 to 1.5
- token_shift: float32 [768], replicated, may hold values from -2 to 2
- char_gain: float32 [768], replicated, may hold values from 0.5 to 1.5
- char_shift: float32 [768], replicated, may hold values from -2 to 2
- token_cot: bfloat16 [4096, 768], P(('dp', 'tensor')), may hold values from -6 to 6
- char_cot: bfloat16 [4096, 768], P(('dp', 'tensor')), may hold values from -6 to 6
Outputs:
- token_out: bfloat16 [4096, 768], P(('dp', 'tensor'))
- char_out: bfloat16 [4096, 768], P(('dp', 'tensor'))
- token_grad: bfloat16 [4096, 768], P(('dp', 'tensor'))
- chars_grad: bfloat16 [16384, 256], P(('dp', 'tensor'))
- grad_qkv_weight: float32 [768, 3, 12, 64], P(None, None, 'tensor')
- grad_qkv_bias: float32 [2, 12, 64], P(None, 'tensor')
- grad_out_weight: float32 [12, 64, 768], P('tensor')
- grad_out_bias: float32 [768], P('tensor')
- grad_attn_gain: float32 [768], P('tensor')
- grad_attn_shift: float32 [768], P('tensor')
- grad_ffn_in_weight: float32 [768, 3072], P(None, 'tensor')
- grad_ffn_in_bias: float32 [3072], P('tensor')
- grad_ffn_out_weight: float32 [3072, 768], P('tensor')
- grad_ffn_out_bias: float32 [768], P('tensor')
- grad_ffn_gain: float32 [768], P('tensor')
- grad_ffn_shift: float32 [768], P('tensor')
- grad_gru_weight: float32 [256, 2, 2, 384], P(None, None, None, 'tensor')
- grad_gate_bias: float32 [2, 384], P(None, 'tensor')
- grad_cand_bias: float32 [2, 384], P(None, 'tensor')
- grad_char_weight: float32 [2, 384, 768], P(None, 'tensor')
- grad_char_bias: float32 [768], P('tensor')
- grad_merge_weight: float32 [3, 1536, 1536], P(None, None, 'tensor')
- grad_merge_bias: float32 [1536], P('tensor')
- grad_token_gain: float32 [768], P('tensor')
- grad_token_shift: float32 [768], P('tensor')
- grad_char_gain: float32 [768], P('tensor')
- grad_char_shift: float32 [768], P('tensor')
The draws below stay inside these ranges and needn't reach their ends.
Inputs may be any that keep to these rules, and one draw needn't show every extreme that they name: `lengths`: each row gives the characters of a sequence's 512 tokens in order; a row sums to 2048. `mask`: 1 marks a token whose character features are dropped.
All inputs are finite; a program needn't handle non-finite values. No bound on the sum of `mask` on one device may be relied on, other than what follows from the above.
Results may differ from the reference program's by a relative error of at most 0.025.
Values may be sent and summed in bfloat16 or wider, within the bound.
No kernel may reach another device: no remote copies, remote signals or barrier semaphores. Data moves between devices by JAX's collectives and lax.ppermute only.
A program may use at most 256 MiB of HBM per device.

```python
import math
import jax
import jax.numpy as jnp
import numpy as np
from jax import lax

D = 768
HEADS = 12
HD = 64
FF = 3072
HGRU = 384
CE = 256
SEQ_LEN = 512
SEQS = 8
TOKENS = 4096
CHAR_LEN = 2048
CHARS = 16384


def with_ends(array, rng, least, top_value):
    spot = [jax.random.randint(jax.random.fold_in(rng, axis), (), 0, length) for axis, length in enumerate(array.shape)]
    longest = array.shape.index(max(array.shape))
    next_to = spot[:longest] + [(spot[longest] + 1) % array.shape[longest]] + spot[longest + 1:]
    return array.at[tuple(spot)].set(least).at[tuple(next_to)].set(top_value)


def steps_of(key, dims, shards, low, high):
    def one(dim, blocks):
        heights = jax.random.uniform(jax.random.fold_in(jax.random.fold_in(key, 6), dim), (blocks,), jnp.float32, low / len(shards), high / len(shards))
        return jnp.repeat(jnp.exp(heights), dims[dim] // blocks).reshape((-1,) + (1,) * (len(dims) - dim - 1))

    loudness = one(*shards[0])
    for cut in shards[1:]:
        loudness = loudness * one(*cut)
    return loudness


def profile(number_of, total, bound, skew):
    loads = [(1 << 20) // math.isqrt(standing ** skew) + 1 for standing in range(2, number_of + 1)]
    surplus, given = total - bound - (number_of - 1), [1] * (number_of - 1)
    while surplus > 0:
        candidates = [i for i in range(number_of - 1) if given[i] < bound]
        mass, budget = sum([loads[i] for i in candidates]), surplus
        for i in candidates:
            addition = min(bound - given[i], max(1, budget * loads[i] // mass), surplus)
            given[i] = given[i] + addition
            surplus = surplus - addition
    return np.array([bound] + given)


def ragged_sizes(key, number_of, total, limit, slope):
    if number_of == 2:
        one = jax.random.randint(key, (), max(1, total - limit), min(limit, total - 1) + 1)
        return jnp.stack([one, total - one])
    sizes = jnp.asarray(profile(number_of, total, limit, slope), jnp.int32)
    pairs = (number_of - 1) // 2
    giver, taker = sizes[1:1 + 2 * pairs:2], sizes[2:2 + 2 * pairs:2]
    room = jnp.minimum(giver - 1, limit - taker)
    moved = jax.random.randint(jax.random.fold_in(key, 1), (pairs,), 0, 1 << 20) % (room + 1)
    sizes = sizes.at[1:1 + 2 * pairs:2].set(giver - moved).at[2:2 + 2 * pairs:2].set(taker + moved)
    return sizes[jax.random.permutation(jax.random.fold_in(key, 2), number_of)]


def bell_draw(rng, shape, width, most, split=(), kind=jnp.bfloat16):
    loudness = steps_of(rng, shape, split, -0.22, 0.18) if split else 1.0
    values = jax.random.normal(rng, shape, jnp.float32) * width * loudness
    return jnp.minimum(jnp.maximum(values, -most), most).astype(kind)


def setup_inputs(seed: int = 0) -> dict:
    arg_keys = jax.random.split(jax.random.key(seed), 30)
    tokens = bell_draw(arg_keys[0], (TOKENS, D), 1.0, 6.0, ((0, 32),))
    chars = bell_draw(arg_keys[1], (CHARS, CE), 1.0, 6.0, ((0, 32),))
    lengths = jax.vmap(lambda own: ragged_sizes(own, SEQ_LEN, CHAR_LEN, 8, 2))(jax.random.split(arg_keys[2], SEQS)).reshape((SEQS, SEQ_LEN)).astype(jnp.int32)
    mask = with_ends((jax.random.randint(arg_keys[3], (SEQS, SEQ_LEN), 0, 8) < 1).astype(jnp.int32), jax.random.fold_in(arg_keys[3], 1), 0, 1)
    qkv_weight = bell_draw(arg_keys[4], (D, 3, HEADS, HD), D ** -0.5, 0.21875, ((2, 4),))
    qkv_bias = bell_draw(arg_keys[5], (2, HEADS, HD), 0.3, 2.0, ((1, 4),), jnp.float32)
    out_weight = bell_draw(arg_keys[6], (HEADS, HD, D), (HEADS * HD // 64) ** -0.5, 1.75, ((0, 4),))
    out_bias = bell_draw(arg_keys[7], (D,), 0.3, 2.0, (), jnp.float32)
    attn_gain = jnp.clip(1.0 + 0.1 * jax.random.normal(arg_keys[8], (D,), jnp.float32), 0.5, 1.5)
    attn_shift = bell_draw(arg_keys[9], (D,), 0.3, 2.0, (), jnp.float32)
    ffn_in_weight = bell_draw(arg_keys[10], (D, FF), D ** -0.5, 0.21875, ((1, 4),))
    ffn_in_bias = bell_draw(arg_keys[11], (FF,), 0.5, 3.0, ((0, 4),), jnp.float32)
    ffn_out_weight = bell_draw(arg_keys[12], (FF, D), (FF // 2) ** -0.5, 0.15625, ((0, 4),))
    ffn_out_bias = bell_draw(arg_keys[13], (D,), 0.3, 2.0, (), jnp.float32)
    ffn_gain = jnp.clip(1.0 + 0.1 * jax.random.normal(arg_keys[14], (D,), jnp.float32), 0.5, 1.5)
    ffn_shift = bell_draw(arg_keys[15], (D,), 0.3, 2.0, (), jnp.float32)
    gru_weight = bell_draw(arg_keys[16], (CE, 2, 2, HGRU), CE ** -0.5, 0.375, ((3, 4),))
    gate_bias = jnp.clip(-6.0 + 6.0 * jax.random.uniform(arg_keys[17], (2, HGRU), jnp.float32) ** steps_of(arg_keys[17], (2, HGRU), ((1, 4),), -0.2, 0.2), -6.0, 0.0)
    cand_bias = bell_draw(arg_keys[18], (2, HGRU), 0.5, 3.0, ((1, 4),), jnp.float32)
    char_weight = bell_draw(arg_keys[19], (2, HGRU, D), (2 * HGRU) ** -0.5, 0.21875, ((1, 4),))
    char_bias = bell_draw(arg_keys[20], (D,), 0.3, 2.0, (), jnp.float32)
    merge_weight = bell_draw(arg_keys[21], (3, 2 * D, 2 * D), (6 * D) ** -0.5, 0.09375, ((2, 4),))
    merge_bias = bell_draw(arg_keys[22], (2 * D,), 0.3, 2.0, ((0, 4),), jnp.float32)
    token_gain = jnp.clip(1.0 + 0.1 * jax.random.normal(arg_keys[23], (D,), jnp.float32), 0.5, 1.5)
    token_shift = bell_draw(arg_keys[24], (D,), 0.3, 2.0, (), jnp.float32)
    char_gain = jnp.clip(1.0 + 0.1 * jax.random.normal(arg_keys[25], (D,), jnp.float32), 0.5, 1.5)
    char_shift = bell_draw(arg_keys[26], (D,), 0.3, 2.0, (), jnp.float32)
    token_cot = bell_draw(arg_keys[27], (TOKENS, D), 1.0, 6.0, ((0, 32),))
    char_cot = bell_draw(arg_keys[28], (TOKENS, D), 1.0, 6.0, ((0, 32),))
    return {"tokens": tokens, "chars": chars, "lengths": lengths, "mask": mask, "qkv_weight": qkv_weight, "qkv_bias": qkv_bias, "out_weight": out_weight, "out_bias": out_bias, "attn_gain": attn_gain, "attn_shift": attn_shift, "ffn_in_weight": ffn_in_weight, "ffn_in_bias": ffn_in_bias, "ffn_out_weight": ffn_out_weight, "ffn_out_bias": ffn_out_bias, "ffn_gain": ffn_gain, "ffn_shift": ffn_shift, "gru_weight": gru_weight, "gate_bias": gate_bias, "cand_bias": cand_bias, "char_weight": char_weight, "char_bias": char_bias, "merge_weight": merge_weight, "merge_bias": merge_bias, "token_gain": token_gain, "token_shift": token_shift, "char_gain": char_gain, "char_shift": char_shift, "token_cot": token_cot, "char_cot": char_cot}


@jax.custom_vjp
def low(v):
    return lax.optimization_barrier(v.astype(jnp.bfloat16)).astype(jnp.float32)

@jax.custom_vjp
def low_back(v):
    return v

def low_keep(v):
    return (low(v), None)

def low_pass(kept, grad):
    return (grad,)

def back_keep(v):
    return (v, None)

def back_low(kept, grad):
    return (low(grad),)
low.defvjp(low_keep, low_pass)
low_back.defvjp(back_keep, back_low)
highest = lax.Precision.HIGHEST
epsilon = 1e-05

def layer_norm(values, gain_vec, shift_vec):
    row_mean = lax.optimization_barrier(jnp.mean(values, axis=-1, keepdims=True))
    centered = values - row_mean
    row_var = lax.optimization_barrier(jnp.mean(centered * centered, axis=-1, keepdims=True))
    return centered * lax.rsqrt(row_var + epsilon) * gain_vec + shift_vec

def combine_pairs(earlier, later):
    return (earlier[0] * later[0], later[0] * earlier[1] + later[1])

def recurrence(decay_rate, drive_term):
    return lax.associative_scan(combine_pairs, (decay_rate, drive_term), axis=0)[1]

def span_bounds(lengths, mask):
    span_ends = jnp.cumsum(lengths, dtype=jnp.int32).astype(jnp.int32) - 1
    starts = (span_ends + 1 - lengths).astype(jnp.int32)
    keep_rows = 1.0 - mask.astype(jnp.float32)
    return (span_ends, starts, keep_rows)

def char_states(gate_values, span_ends, starts, keep_rows):
    update = jax.nn.sigmoid(gate_values[:, 0])
    drive_term = update * gate_values[:, 1]
    forward = recurrence(1.0 - update[:, 0], drive_term[:, 0])
    backward = jnp.flip(recurrence(jnp.flip(1.0 - update[:, 1], 0), jnp.flip(drive_term[:, 1], 0)), 0)
    pooled = jnp.stack([forward[span_ends], backward[starts]], axis=1) * keep_rows[:, None, None]
    return pooled.reshape(pooled.shape[0], -1)

def sequence_layer(params, tok_seq, chr_seq, lengths, mask):
    qkv_weight, qkv_bias, out_weight, out_bias, attn_gain, attn_shift, ffn_in_weight, ffn_in_bias, ffn_out_weight, ffn_out_bias, ffn_gain, ffn_shift, gru_weight, gate_bias, cand_bias, char_weight, char_bias, merge_weight, merge_bias, token_gain, token_shift, char_gain, char_shift = params
    seq_rows = tok_seq.shape[0]
    projected = jnp.dot(tok_seq, qkv_weight.reshape(D, -1), precision=highest).reshape(seq_rows, 3, HEADS, HD)
    queries = low(low_back((projected[:, 0] + qkv_bias[0]) * 0.125))
    key_rows = low(low_back(projected[:, 1]))
    values = low(low_back(projected[:, 2] + qkv_bias[1]))
    scores = low_back(jnp.einsum('qhd,khd->hqk', queries, key_rows, precision=highest))
    probs_low = low(jax.nn.softmax(scores, axis=-1))
    mixed = low(low_back(jnp.einsum('hqk,khd->qhd', probs_low, values, precision=highest)))
    attn_out = low_back(jnp.dot(mixed.reshape(seq_rows, -1), out_weight.reshape(-1, D), precision=highest) + out_bias)
    first_out = layer_norm(tok_seq + attn_out, attn_gain, attn_shift)
    first_low = low(first_out)
    hidden_pre = low_back(jnp.dot(first_low, ffn_in_weight, precision=highest) + ffn_in_bias)
    inter = low(jax.nn.gelu(hidden_pre, approximate=False))
    ffn_out = low_back(jnp.dot(inter, ffn_out_weight, precision=highest) + ffn_out_bias)
    second_out = layer_norm(first_out + ffn_out, ffn_gain, ffn_shift)
    span_ends, starts, keep_rows = span_bounds(lengths, mask)
    unit_count = gru_weight.shape[3]
    gate_values = jnp.dot(chr_seq, gru_weight.reshape(CE, -1), precision=highest).reshape(-1, 2, 2, unit_count)
    gate_values = low_back(gate_values + jnp.stack([gate_bias, cand_bias]))
    pooled = low(char_states(gate_values, span_ends, starts, keep_rows))
    char_mid = low_back(jnp.dot(pooled, char_weight.reshape(-1, D), precision=highest) + char_bias)
    joined = jnp.concatenate([low(second_out), low(char_mid)], axis=1)
    padded = jnp.pad(joined, ((1, 1), (0, 0)))
    merged = merge_bias + jnp.dot(padded[0:seq_rows], merge_weight[0], precision=highest)
    merged = merged + jnp.dot(padded[1:1 + seq_rows], merge_weight[1], precision=highest)
    merged = merged + jnp.dot(padded[2:2 + seq_rows], merge_weight[2], precision=highest)
    merged = low(low_back(merged))
    token_out = layer_norm(second_out + merged[:, :D], token_gain, token_shift)
    char_out = layer_norm(char_mid + merged[:, D:], char_gain, char_shift)
    return (token_out, char_out)

def reference(tokens, chars, lengths, mask, qkv_weight, qkv_bias, out_weight, out_bias, attn_gain, attn_shift, ffn_in_weight, ffn_in_bias, ffn_out_weight, ffn_out_bias, ffn_gain, ffn_shift, gru_weight, gate_bias, cand_bias, char_weight, char_bias, merge_weight, merge_bias, token_gain, token_shift, char_gain, char_shift, token_cot, char_cot):
    params = tuple((member.astype(jnp.float32) for member in (qkv_weight, qkv_bias, out_weight, out_bias, attn_gain, attn_shift, ffn_in_weight, ffn_in_bias, ffn_out_weight, ffn_out_bias, ffn_gain, ffn_shift, gru_weight, gate_bias, cand_bias, char_weight, char_bias, merge_weight, merge_bias, token_gain, token_shift, char_gain, char_shift)))
    tok_seq = tokens.astype(jnp.float32).reshape(SEQS, SEQ_LEN, D)
    chr_seq = chars.astype(jnp.float32).reshape(SEQS, CHAR_LEN, CE)

    def forward(weights, tok_all, chr_all):

        def one_sequence(item_tuple):
            return jax.checkpoint(sequence_layer)(weights, *item_tuple)
        return lax.map(one_sequence, (tok_all, chr_all, lengths, mask))
    outputs, pull_back = jax.vjp(forward, params, tok_seq, chr_seq)
    cot_pair = (token_cot.astype(jnp.float32).reshape(SEQS, SEQ_LEN, D), char_cot.astype(jnp.float32).reshape(SEQS, SEQ_LEN, D))
    grad_params, grad_tokens, grad_chars = pull_back(cot_pair)
    return (outputs[0].reshape(TOKENS, D).astype(jnp.bfloat16), outputs[1].reshape(TOKENS, D).astype(jnp.bfloat16), grad_tokens.reshape(TOKENS, D).astype(jnp.bfloat16), grad_chars.reshape(CHARS, CE).astype(jnp.bfloat16), grad_params[0], grad_params[1], grad_params[2], grad_params[3], grad_params[4], grad_params[5], grad_params[6], grad_params[7], grad_params[8], grad_params[9], grad_params[10], grad_params[11], grad_params[12], grad_params[13], grad_params[14], grad_params[15], grad_params[16], grad_params[17], grad_params[18], grad_params[19], grad_params[20], grad_params[21], grad_params[22])
```

```python
import jax
import jax.numpy as jnp
from jax import lax
from jax.experimental import pallas as pl
from jax.experimental.pallas import tpu as pltpu
from jax.sharding import PartitionSpec as P

D = 768
HD = 64
CE = 256
epsilon = 1e-05
F32 = jnp.float32
BF16 = jnp.bfloat16
LANES = 128
SEGS = 32
CHUNK = 256


def full_call(kernel, outs, scratch, flops, *args):
    vmem = pl.BlockSpec(memory_space=pltpu.VMEM)
    return pl.pallas_call(
        kernel,
        out_shape=outs,
        in_specs=[vmem] * len(args),
        out_specs=[vmem] * len(outs),
        scratch_shapes=scratch,
        cost_estimate=pl.CostEstimate(
            flops=flops,
            transcendentals=0,
            bytes_accessed=sum(a.size * a.dtype.itemsize for a in args)
            + sum(o.size * o.dtype.itemsize for o in outs),
        ),
    )(*args)


def dot_nn(a, b):
    return lax.dot_general(a, b, (((1,), (0,)), ((), ())), preferred_element_type=F32)


def dot_nt(a, b):
    return lax.dot_general(a, b, (((1,), (1,)), ((), ())), preferred_element_type=F32)


def dot_tn(a, b):
    return lax.dot_general(a, b, (((0,), (0,)), ((), ())), preferred_element_type=F32)


def gru_forward_kernel(
    chr_ref, w_ref, b_ref, len_ref, mask_ref, cw_ref,
    u_ref, e_ref, pooled_ref, part_ref,
    uf, ub, cf, cb, hf, hb, pend, hend, hin,
):
    rows = chr_ref.shape[0]
    count = len_ref.shape[1]
    steps = rows // SEGS

    def gates(i, _):
        at = pl.ds(i * CHUNK, CHUNK)
        g = dot_nn(chr_ref[at, :], w_ref[...]) + b_ref[...]
        u = jax.nn.sigmoid(g[:, : 2 * LANES])
        u_ref[at, :] = u
        uf[at, :] = u[:, :LANES]
        ub[at, :] = u[:, LANES:]
        cf[at, :] = g[:, 2 * LANES : 3 * LANES]
        cb[at, :] = g[:, 3 * LANES :]
        return 0

    lax.fori_loop(0, rows // CHUNK, gates, 0)
    ones = jnp.ones((SEGS, LANES), F32)
    zeros = jnp.zeros((SEGS, LANES), F32)

    def at_step(step):
        return pl.ds(step, SEGS, stride=steps)

    def local(step, carry):
        h_f, p_f, h_b, p_b = carry
        at_f, at_b = at_step(step), at_step(steps - 1 - step)
        u = uf[at_f, :]
        a = 1.0 - u
        h_f = a * h_f + u * cf[at_f, :]
        p_f = a * p_f
        u = ub[at_b, :]
        a = 1.0 - u
        h_b = a * h_b + u * cb[at_b, :]
        p_b = a * p_b
        return h_f, p_f, h_b, p_b

    h_f, p_f, h_b, p_b = lax.fori_loop(0, steps, local, (zeros, ones, zeros, ones), unroll=2)
    hend[:, :LANES] = h_f
    hend[:, LANES:] = h_b
    pend[:, :LANES] = p_f
    pend[:, LANES:] = p_b
    one_f = jnp.zeros((1, LANES), F32)
    one_b = jnp.zeros((1, LANES), F32)
    for s in range(SEGS):
        r = SEGS - 1 - s
        hin[s : s + 1, :LANES] = one_f
        hin[r : r + 1, LANES:] = one_b
        one_f = pend[s : s + 1, :LANES] * one_f + hend[s : s + 1, :LANES]
        one_b = pend[r : r + 1, LANES:] * one_b + hend[r : r + 1, LANES:]

    def final(step, carry):
        h_f, h_b = carry
        at_f, at_b = at_step(step), at_step(steps - 1 - step)
        e = cf[at_f, :] - h_f
        cf[at_f, :] = e
        h_f = h_f + uf[at_f, :] * e
        hf[at_f, :] = h_f
        e = cb[at_b, :] - h_b
        cb[at_b, :] = e
        h_b = h_b + ub[at_b, :] * e
        hb[at_b, :] = h_b
        return h_f, h_b

    lax.fori_loop(0, steps, final, (hin[:, :LANES], hin[:, LANES:]), unroll=2)
    e_ref[:, :LANES] = cf[...]
    e_ref[:, LANES:] = cb[...]
    row_i = lax.broadcasted_iota(jnp.int32, (count, count), 0)
    col_i = lax.broadcasted_iota(jnp.int32, (count, count), 1)
    lens = len_ref[...].astype(F32)
    drop = mask_ref[...].astype(F32) * (-2.0 * rows)
    own = jnp.where(row_i == col_i, drop, 0.0)
    ends = jnp.sum(jnp.where(col_i <= row_i, lens, 0.0) + own, axis=1, keepdims=True) - 1.0
    starts = jnp.sum(jnp.where(col_i < row_i, lens, 0.0) + own, axis=1, keepdims=True)
    iota = lax.broadcasted_iota(jnp.int32, (count, CHUNK), 1).astype(F32)
    acc_f = jnp.zeros((count, LANES), F32)
    acc_b = jnp.zeros((count, LANES), F32)
    for i in range(rows // CHUNK):
        pick = jnp.where(iota == ends - float(i * CHUNK), 1.0, 0.0).astype(BF16)
        acc_f = acc_f + dot_nn(pick, hf[i * CHUNK : (i + 1) * CHUNK, :].astype(BF16))
        pick = jnp.where(iota == starts - float(i * CHUNK), 1.0, 0.0).astype(BF16)
        acc_b = acc_b + dot_nn(pick, hb[i * CHUNK : (i + 1) * CHUNK, :].astype(BF16))
    pooled = jnp.concatenate([acc_f.astype(BF16), acc_b.astype(BF16)], axis=1)
    pooled_ref[...] = pooled
    part_ref[...] = dot_nn(pooled, cw_ref[...]).astype(BF16)


def gru_forward(chr_all, w, b, lengths, mask, cw):
    rows, count = chr_all.shape[0], lengths.shape[1]
    outs = [
        jax.ShapeDtypeStruct((rows, 2 * LANES), F32),
        jax.ShapeDtypeStruct((rows, 2 * LANES), F32),
        jax.ShapeDtypeStruct((count, 2 * LANES), BF16),
        jax.ShapeDtypeStruct((count, cw.shape[1]), BF16),
    ]
    scratch = [pltpu.VMEM((rows, LANES), F32)] * 6 + [pltpu.VMEM((SEGS, 2 * LANES), F32)] * 3
    flops = 2 * rows * chr_all.shape[1] * 4 * LANES + 4 * rows * count * LANES
    return full_call(
        gru_forward_kernel, outs, scratch, flops, chr_all, w, b, lengths, mask, cw
    )


def gru_backward_kernel(
    gmid_ref, cw_ref, pooled_ref, u_ref, e_ref, chr_ref, w_ref, len_ref, mask_ref,
    gchr_ref, gw_ref, gb_ref, gcw_ref,
    uf, ub, ef, eb, gf, gb, pend, hend, hin,
):
    rows = chr_ref.shape[0]
    count = len_ref.shape[1]
    steps = rows // SEGS
    gcw_ref[...] = dot_tn(pooled_ref[...], gmid_ref[...]).astype(gcw_ref.dtype)
    g_pooled = dot_nt(gmid_ref[...], cw_ref[...]).astype(BF16)
    row_i = lax.broadcasted_iota(jnp.int32, (count, count), 0)
    col_i = lax.broadcasted_iota(jnp.int32, (count, count), 1)
    upper = jnp.where(row_i <= col_i, 1.0, 0.0).astype(BF16)
    lens = len_ref[...].astype(F32)
    drop = mask_ref[...].astype(F32) * (-2.0 * rows)
    ends = dot_nn(lens.astype(BF16), upper) - 1.0
    starts = ends + 1.0 - lens + drop
    ends = ends + drop
    iota = lax.broadcasted_iota(jnp.int32, (CHUNK, count), 0).astype(F32)

    def spread(i, _):
        at = pl.ds(i * CHUNK, CHUNK)
        base = (i * CHUNK).astype(F32)
        pick = jnp.where(iota == ends - base, 1.0, 0.0).astype(BF16)
        gf[at, :] = dot_nn(pick, g_pooled[:, :LANES])
        pick = jnp.where(iota == starts - base, 1.0, 0.0).astype(BF16)
        gb[at, :] = dot_nn(pick, g_pooled[:, LANES:])
        return 0

    lax.fori_loop(0, rows // CHUNK, spread, 0)
    uf[...] = u_ref[:, :LANES]
    ub[...] = u_ref[:, LANES:]
    ef[...] = e_ref[:, :LANES]
    eb[...] = e_ref[:, LANES:]
    ones = jnp.ones((SEGS, LANES), F32)
    zeros = jnp.zeros((SEGS, LANES), F32)

    def at_step(step):
        return pl.ds(step, SEGS, stride=steps)

    def local(step, carry):
        x_f, p_f, x_b, p_b = carry
        at_f, at_b = at_step(steps - 1 - step), at_step(step)
        a = 1.0 - uf[at_f, :]
        x_f = a * (gf[at_f, :] + x_f)
        p_f = a * p_f
        a = 1.0 - ub[at_b, :]
        x_b = a * (gb[at_b, :] + x_b)
        p_b = a * p_b
        return x_f, p_f, x_b, p_b

    x_f, p_f, x_b, p_b = lax.fori_loop(0, steps, local, (zeros, ones, zeros, ones), unroll=2)
    hend[:, :LANES] = x_f
    hend[:, LANES:] = x_b
    pend[:, :LANES] = p_f
    pend[:, LANES:] = p_b
    one_f = jnp.zeros((1, LANES), F32)
    one_b = jnp.zeros((1, LANES), F32)
    for s in range(SEGS):
        r = SEGS - 1 - s
        hin[r : r + 1, :LANES] = one_f
        hin[s : s + 1, LANES:] = one_b
        one_f = pend[r : r + 1, :LANES] * one_f + hend[r : r + 1, :LANES]
        one_b = pend[s : s + 1, LANES:] * one_b + hend[s : s + 1, LANES:]

    def final(step, carry):
        x_f, x_b = carry
        at_f, at_b = at_step(steps - 1 - step), at_step(step)
        u = uf[at_f, :]
        a = 1.0 - u
        d = gf[at_f, :] + x_f
        gf[at_f, :] = d * u
        x_f = a * d
        ef[at_f, :] = ef[at_f, :] * (u * x_f)
        u = ub[at_b, :]
        a = 1.0 - u
        d = gb[at_b, :] + x_b
        gb[at_b, :] = d * u
        x_b = a * d
        eb[at_b, :] = eb[at_b, :] * (u * x_b)
        return x_f, x_b

    lax.fori_loop(0, steps, final, (hin[:, :LANES], hin[:, LANES:]), unroll=2)
    gw_acc = jnp.zeros(gw_ref.shape, F32)
    gb_acc = jnp.zeros((1, 4 * LANES), F32)
    for i in range(rows // CHUNK):
        at = slice(i * CHUNK, (i + 1) * CHUNK)
        gates = jnp.concatenate([ef[at, :], eb[at, :], gf[at, :], gb[at, :]], axis=1).astype(BF16)
        gb_acc = gb_acc + jnp.sum(gates.astype(F32), axis=0, keepdims=True)
        gchr_ref[at, :] = dot_nt(gates, w_ref[...]).astype(BF16)
        gw_acc = gw_acc + dot_tn(chr_ref[at, :], gates)
    gw_ref[...] = gw_acc.astype(gw_ref.dtype)
    gb_ref[...] = gb_acc


def gru_backward(g_mid, cw, pooled, u, e, chr_all, w, lengths, mask):
    rows, count = chr_all.shape[0], lengths.shape[1]
    outs = [
        jax.ShapeDtypeStruct(chr_all.shape, BF16),
        jax.ShapeDtypeStruct(w.shape, BF16),
        jax.ShapeDtypeStruct((1, 4 * LANES), F32),
        jax.ShapeDtypeStruct(cw.shape, BF16),
    ]
    scratch = [pltpu.VMEM((rows, LANES), F32)] * 6 + [pltpu.VMEM((SEGS, 2 * LANES), F32)] * 3
    flops = 4 * rows * chr_all.shape[1] * 4 * LANES + 4 * rows * count * LANES
    return full_call(
        gru_backward_kernel, outs, scratch, flops,
        g_mid, cw, pooled, u, e, chr_all, w, lengths, mask,
    )


def pad_units(array, axis):
    wide = [(0, 0)] * array.ndim
    wide[axis] = (0, LANES - array.shape[axis])
    return jnp.pad(array, wide)


def layer_norm(values, gain_vec, shift_vec):
    row_mean = jnp.mean(values, axis=-1, keepdims=True)
    centered = values - row_mean
    row_var = jnp.mean(centered * centered, axis=-1, keepdims=True)
    return centered * lax.rsqrt(row_var + epsilon) * gain_vec + shift_vec


def gelu_exact(values):
    return jax.nn.gelu(values, approximate=False)


def rounded(values):
    return values.astype(jnp.bfloat16)


def body(
    tokens,
    chars,
    lengths,
    mask,
    qkv_weight,
    qkv_bias,
    out_weight,
    out_bias,
    attn_gain,
    attn_shift,
    ffn_in_weight,
    ffn_in_bias,
    ffn_out_weight,
    ffn_out_bias,
    ffn_gain,
    ffn_shift,
    gru_weight,
    gate_bias,
    cand_bias,
    char_weight,
    char_bias,
    merge_weight,
    merge_bias,
    token_gain,
    token_shift,
    char_gain,
    char_shift,
    token_cot,
    char_cot,
):
    tok_all, chr_all = (
        lax.all_gather(tokens, "tensor", axis=0, tiled=True),
        lax.all_gather(chars, "tensor", axis=0, tiled=True),
    )
    seq_rows = tok_all.shape[0]
    head_count = qkv_weight.shape[2]
    unit_count = gru_weight.shape[3]
    projected = jnp.dot(
        tok_all, qkv_weight.reshape(D, -1), preferred_element_type=jnp.float32
    ).reshape(seq_rows, 3, head_count, HD)
    queries = rounded((projected[:, 0] + qkv_bias[0]) * 0.125)
    key_rows = rounded(projected[:, 1])
    values = rounded(projected[:, 2] + qkv_bias[1])
    scores = jnp.einsum("qhd,khd->hqk", queries, key_rows, preferred_element_type=jnp.float32)
    maxima = jnp.max(scores, axis=-1, keepdims=True)
    totals = jnp.sum(jnp.exp(scores - maxima), axis=-1, keepdims=True)
    log_norm = maxima + jnp.log(totals)
    probs_low = rounded(jnp.exp(scores - log_norm))
    mixed = rounded(
        jnp.einsum("hqk,khd->qhd", probs_low, values, preferred_element_type=jnp.float32)
    ).reshape(seq_rows, head_count * HD)
    attn_part = jnp.dot(mixed, out_weight.reshape(-1, D), preferred_element_type=jnp.float32)
    wide_gru = pad_units(gru_weight, 3).reshape(CE, -1)
    wide_bias = pad_units(jnp.stack([gate_bias, cand_bias]), 2).reshape(1, -1)
    wide_char = pad_units(char_weight, 1).reshape(-1, D)
    update, excess, pooled_low, char_part = gru_forward(
        chr_all, wide_gru, wide_bias, lengths, mask, wide_char
    )
    attn_rows = lax.psum_scatter(
        attn_part.astype(jnp.bfloat16), "tensor", scatter_dimension=0, tiled=True
    ).astype(jnp.float32)
    first_in_own = tokens.astype(jnp.float32) + attn_rows + out_bias
    first_out, first_pull = jax.vjp(layer_norm, first_in_own, attn_gain, attn_shift)
    first_low_all = lax.all_gather(rounded(first_out), "tensor", axis=0, tiled=True)
    hidden_pre = (
        jnp.dot(first_low_all, ffn_in_weight, preferred_element_type=jnp.float32) + ffn_in_bias
    )
    inter_full, gelu_pull = jax.vjp(gelu_exact, hidden_pre)
    inter_low = rounded(inter_full)
    ffn_part = jnp.dot(inter_low, ffn_out_weight, preferred_element_type=jnp.float32)
    ffn_sum, char_sum = (
        lax.psum_scatter(
            ffn_part.astype(jnp.bfloat16), "tensor", scatter_dimension=0, tiled=True
        ).astype(jnp.float32),
        lax.psum_scatter(
            char_part, "tensor", scatter_dimension=0, tiled=True
        ).astype(jnp.float32),
    )
    second_out, second_pull = jax.vjp(
        layer_norm, first_out + ffn_sum + ffn_out_bias, ffn_gain, ffn_shift
    )
    char_mid = char_sum + char_bias
    second_all, mid_all = (
        lax.all_gather(rounded(second_out), "tensor", axis=0, tiled=True),
        lax.all_gather(rounded(char_mid), "tensor", axis=0, tiled=True),
    )
    padded = jnp.pad(jnp.concatenate([second_all, mid_all], axis=1), ((1, 1), (0, 0)))
    merged_cols = merge_bias + jnp.dot(
        padded[0:seq_rows], merge_weight[0], preferred_element_type=jnp.float32
    )
    merged_cols = merged_cols + jnp.dot(
        padded[1 : 1 + seq_rows], merge_weight[1], preferred_element_type=jnp.float32
    )
    merged_cols = merged_cols + jnp.dot(
        padded[2 : 2 + seq_rows], merge_weight[2], preferred_element_type=jnp.float32
    )
    merged = lax.all_to_all(
        rounded(merged_cols), "tensor", split_axis=0, concat_axis=1, tiled=True
    ).astype(jnp.float32)
    token_out, token_pull = jax.vjp(layer_norm, second_out + merged[:, :D], token_gain, token_shift)
    char_out, char_pull = jax.vjp(layer_norm, char_mid + merged[:, D:], char_gain, char_shift)
    g_token, grad_token_gain, grad_token_shift = token_pull(token_cot.astype(jnp.float32))
    g_char, grad_char_gain, grad_char_shift = char_pull(char_cot.astype(jnp.float32))
    g_cols = lax.all_to_all(
        rounded(jnp.concatenate([g_token, g_char], axis=1)),
        "tensor",
        split_axis=1,
        concat_axis=0,
        tiled=True,
    )
    grad_merge_bias = jnp.sum(g_cols.astype(jnp.float32), axis=0)
    grad_merge_weight = jnp.stack(
        [
            jnp.einsum(
                "ti,to->io",
                padded[offset : offset + seq_rows],
                g_cols,
                preferred_element_type=jnp.float32,
            )
            for offset in range(3)
        ]
    )
    g_padded = jnp.pad(g_cols, ((1, 1), (0, 0)))
    g_joined = jnp.einsum(
        "to,io->ti", g_padded[2 : 2 + seq_rows], merge_weight[0], preferred_element_type=jnp.float32
    )
    g_joined = g_joined + jnp.einsum(
        "to,io->ti", g_padded[1 : 1 + seq_rows], merge_weight[1], preferred_element_type=jnp.float32
    )
    g_joined = g_joined + jnp.einsum(
        "to,io->ti", g_padded[0:seq_rows], merge_weight[2], preferred_element_type=jnp.float32
    )
    g_rows = lax.psum_scatter(
        g_joined.astype(jnp.bfloat16), "tensor", scatter_dimension=0, tiled=True
    ).astype(jnp.float32)
    g_second = g_token + g_rows[:, :D]
    g_mid_low = rounded(g_char + g_rows[:, D:])
    ffn_in_grad, grad_ffn_gain, grad_ffn_shift = second_pull(g_second)
    ffn_grad_low = rounded(ffn_in_grad)
    grad_ffn_out_bias = jnp.sum(ffn_grad_low.astype(jnp.float32), axis=0)
    grad_char_bias = jnp.sum(g_mid_low.astype(jnp.float32), axis=0)
    ffn_grad_all, g_mid_all = (
        lax.all_gather(ffn_grad_low, "tensor", axis=0, tiled=True),
        lax.all_gather(g_mid_low, "tensor", axis=0, tiled=True),
    )
    grad_ffn_out_weight = jnp.einsum(
        "tf,td->fd", inter_low, ffn_grad_all, preferred_element_type=jnp.float32
    )
    inter_grad = jnp.einsum(
        "td,fd->tf", ffn_grad_all, ffn_out_weight, preferred_element_type=jnp.float32
    )
    hidden_grad = rounded(gelu_pull(inter_grad)[0])
    grad_ffn_in_bias = jnp.sum(hidden_grad.astype(jnp.float32), axis=0)
    grad_ffn_in_weight = jnp.einsum(
        "tc,tf->cf", first_low_all, hidden_grad, preferred_element_type=jnp.float32
    )
    first_part = jnp.einsum(
        "tf,cf->tc", hidden_grad, ffn_in_weight, preferred_element_type=jnp.float32
    )
    g_chr_all, wide_gru_grad, wide_bias_grad, wide_char_grad = gru_backward(
        g_mid_all, wide_char, pooled_low, update, excess, chr_all, wide_gru, lengths, mask
    )
    grad_gru_weight = wide_gru_grad.reshape(CE, 2, 2, LANES)[..., :unit_count]
    wide_bias_grad = wide_bias_grad.reshape(2, 2, LANES)[..., :unit_count]
    grad_gate_bias, grad_cand_bias = wide_bias_grad[0], wide_bias_grad[1]
    grad_char_weight = wide_char_grad.reshape(2, LANES, D)[:, :unit_count]
    first_rows = lax.psum_scatter(
        first_part.astype(jnp.bfloat16), "tensor", scatter_dimension=0, tiled=True
    ).astype(jnp.float32)
    first_grad = ffn_in_grad + first_rows
    g_resid, grad_attn_gain, grad_attn_shift = first_pull(first_grad)
    g_attn_low = rounded(g_resid)
    grad_out_bias = jnp.sum(g_attn_low.astype(jnp.float32), axis=0)
    g_attn_all = lax.all_gather(g_attn_low, "tensor", axis=0, tiled=True)
    grad_out_weight = jnp.einsum(
        "tk,td->kd", mixed, g_attn_all, preferred_element_type=jnp.float32
    ).reshape(out_weight.shape)
    g_mixed = rounded(
        jnp.einsum(
            "td,kd->tk", g_attn_all, out_weight.reshape(-1, D), preferred_element_type=jnp.float32
        )
    ).reshape(seq_rows, head_count, HD)
    scores_again = jnp.einsum("qhd,khd->hqk", queries, key_rows, preferred_element_type=jnp.float32)
    probs_again = jnp.exp(scores_again - log_norm)
    probs_again_low = rounded(probs_again)
    g_values = jnp.einsum(
        "hqk,qhd->khd", probs_again_low, g_mixed, preferred_element_type=jnp.float32
    )
    g_probs = jnp.einsum("qhd,khd->hqk", g_mixed, values, preferred_element_type=jnp.float32)
    g_scores = rounded(
        probs_again * (g_probs - jnp.sum(g_probs * probs_again, axis=-1, keepdims=True))
    )
    g_queries = jnp.einsum("hqk,khd->qhd", g_scores, key_rows, preferred_element_type=jnp.float32)
    g_keys = jnp.einsum("hqk,qhd->khd", g_scores, queries, preferred_element_type=jnp.float32)
    g_project = jnp.stack([rounded(g_queries) * 0.125, rounded(g_keys), rounded(g_values)], axis=1)
    g_flat = g_project.reshape(seq_rows, -1)
    grad_qkv_weight = jnp.einsum(
        "tc,tf->cf", tok_all, g_flat, preferred_element_type=jnp.float32
    ).reshape(qkv_weight.shape)
    grad_qkv_bias = jnp.stack(
        [
            jnp.sum(g_project[:, 0].astype(jnp.float32), axis=0),
            jnp.sum(g_project[:, 2].astype(jnp.float32), axis=0),
        ]
    )
    g_tok_all = jnp.einsum(
        "tf,cf->tc", g_flat, qkv_weight.reshape(D, -1), preferred_element_type=jnp.float32
    )
    norm_parts = jnp.stack(
        [
            grad_out_bias,
            grad_attn_gain,
            grad_attn_shift,
            grad_ffn_out_bias,
            grad_ffn_gain,
            grad_ffn_shift,
            grad_char_bias,
            grad_token_gain,
            grad_token_shift,
            grad_char_gain,
            grad_char_shift,
        ]
    )
    g_tok_rows, g_chr_rows, norm_rows = (
        lax.psum_scatter(
            g_tok_all.astype(jnp.bfloat16), "tensor", scatter_dimension=0, tiled=True
        ).astype(jnp.float32),
        lax.psum_scatter(
            g_chr_all, "tensor", scatter_dimension=0, tiled=True
        ).astype(jnp.float32),
        lax.psum_scatter(
            norm_parts.astype(jnp.bfloat16), "tensor", scatter_dimension=1, tiled=True
        ).astype(jnp.float32),
    )
    token_grad = rounded(g_resid + g_tok_rows)
    chars_grad = rounded(g_chr_rows)
    def over_sequences(*parts):
        return [
            total.astype(jnp.float32)
            for total in lax.psum(tuple(part.astype(jnp.bfloat16) for part in parts), "dp")
        ]

    (
        grad_qkv_weight,
        grad_out_weight,
        grad_gru_weight,
        grad_char_weight,
        grad_merge_weight,
        grad_ffn_in_weight,
        grad_ffn_out_weight,
    ) = over_sequences(
        grad_qkv_weight,
        grad_out_weight,
        grad_gru_weight,
        grad_char_weight,
        grad_merge_weight,
        grad_ffn_in_weight,
        grad_ffn_out_weight,
    )
    (
        grad_qkv_bias,
        grad_gate_bias,
        grad_cand_bias,
        grad_merge_bias,
        grad_ffn_in_bias,
        norm_rows,
    ) = lax.psum(
        (
            grad_qkv_bias,
            grad_gate_bias,
            grad_cand_bias,
            grad_merge_bias,
            grad_ffn_in_bias,
            norm_rows,
        ),
        "dp",
    )
    return (
        rounded(token_out),
        rounded(char_out),
        token_grad,
        chars_grad,
        grad_qkv_weight,
        grad_qkv_bias,
        grad_out_weight,
        norm_rows[0],
        norm_rows[1],
        norm_rows[2],
        grad_ffn_in_weight,
        grad_ffn_in_bias,
        grad_ffn_out_weight,
        norm_rows[3],
        norm_rows[4],
        norm_rows[5],
        grad_gru_weight,
        grad_gate_bias,
        grad_cand_bias,
        grad_char_weight,
        norm_rows[6],
        grad_merge_weight,
        grad_merge_bias,
        norm_rows[7],
        norm_rows[8],
        norm_rows[9],
        norm_rows[10],
    )


def solution(mesh):
    in_specs = (
        P(("dp", "tensor"), None),
        P(("dp", "tensor"), None),
        P("dp", None),
        P("dp", None),
        P(None, None, "tensor", None),
        P(None, "tensor", None),
        P("tensor", None, None),
        P(),
        P(),
        P(),
        P(None, "tensor"),
        P("tensor"),
        P("tensor", None),
        P(),
        P(),
        P(),
        P(None, None, None, "tensor"),
        P(None, "tensor"),
        P(None, "tensor"),
        P(None, "tensor", None),
        P(),
        P(None, None, "tensor"),
        P("tensor"),
        P(),
        P(),
        P(),
        P(),
        P(("dp", "tensor"), None),
        P(("dp", "tensor"), None),
    )
    out_specs = (
        P(("dp", "tensor"), None),
        P(("dp", "tensor"), None),
        P(("dp", "tensor"), None),
        P(("dp", "tensor"), None),
        P(None, None, "tensor", None),
        P(None, "tensor", None),
        P("tensor", None, None),
        P("tensor"),
        P("tensor"),
        P("tensor"),
        P(None, "tensor"),
        P("tensor"),
        P("tensor", None),
        P("tensor"),
        P("tensor"),
        P("tensor"),
        P(None, None, None, "tensor"),
        P(None, "tensor"),
        P(None, "tensor"),
        P(None, "tensor", None),
        P("tensor"),
        P(None, None, "tensor"),
        P("tensor"),
        P("tensor"),
        P("tensor"),
        P("tensor"),
        P("tensor"),
    )
    return jax.shard_map(body, mesh=mesh, in_specs=in_specs, out_specs=out_specs, check_vma=False)
```

```python
import math

import jax
import jax.numpy as jnp
from jax import lax
from jax.experimental import pallas as pl
from jax.experimental.pallas import tpu as pltpu
from jax.sharding import PartitionSpec as P

D = 768
HD = 64
CE = 256
epsilon = 1e-05
F32 = jnp.float32
BF16 = jnp.bfloat16
LANES = 128
SEGS = 32
CHUNK = 256
ORDER = (0, 2, 1, 3)


def full_call(kernel, outs, scratch, flops, *args):
    vmem = pl.BlockSpec(memory_space=pltpu.VMEM)
    smem = pl.BlockSpec(memory_space=pltpu.SMEM)
    return pl.pallas_call(
        kernel,
        out_shape=[jax.ShapeDtypeStruct(shape, kind) for shape, kind in outs],
        in_specs=[smem if a.shape == (1,) else vmem for a in args],
        out_specs=[vmem] * len(outs),
        scratch_shapes=[pltpu.VMEM(shape, kind) for shape, kind in scratch],
        cost_estimate=pl.CostEstimate(
            flops=int(flops),
            transcendentals=0,
            bytes_accessed=sum(a.size * a.dtype.itemsize for a in args)
            + sum(jnp.dtype(kind).itemsize * math.prod(shape) for shape, kind in outs),
        ),
    )(*args)


def dot_nn(a, b):
    return lax.dot_general(a, b, (((1,), (0,)), ((), ())), preferred_element_type=F32)


def dot_nt(a, b):
    return lax.dot_general(a, b, (((1,), (1,)), ((), ())), preferred_element_type=F32)


def dot_tn(a, b):
    return lax.dot_general(a, b, (((0,), (0,)), ((), ())), preferred_element_type=F32)


def rows_at(me, k, size):
    return pl.ds(pl.multiple_of((me ^ ORDER[k]) * size, size), size)


def bounds_columns(len_ref, mask_ref, rows):
    count = len_ref.shape[1]
    row_i = lax.broadcasted_iota(jnp.int32, (count, count), 0)
    col_i = lax.broadcasted_iota(jnp.int32, (count, count), 1)
    lens = len_ref[...].astype(F32)
    drop = mask_ref[...].astype(F32) * (-2.0 * rows)
    own = jnp.where(row_i == col_i, drop, 0.0)
    ends = jnp.sum(jnp.where(col_i <= row_i, lens, 0.0) + own, axis=1, keepdims=True) - 1.0
    starts = jnp.sum(jnp.where(col_i < row_i, lens, 0.0) + own, axis=1, keepdims=True)
    return ends, starts


def gru_forward_kernel(
    me_ref, c0, c1, c2, c3, w_ref, b_ref, len_ref, mask_ref, cw_ref,
    u_ref, e_ref, pooled_ref, part_a, part_b,
    uf, ub, cf, cb, hf, hb, pend, hend, hin,
):
    me = me_ref[0]
    rows = 4 * c0.shape[0]
    count = len_ref.shape[1]
    steps = rows // SEGS
    for k, c_ref in enumerate((c0, c1, c2, c3)):
        for half in range(c0.shape[0] // CHUNK):
            start = pl.multiple_of((me ^ ORDER[k]) * c0.shape[0] + half * CHUNK, CHUNK)
            at = pl.ds(start, CHUNK)
            g = dot_nn(c_ref[half * CHUNK : (half + 1) * CHUNK, :], w_ref[...]) + b_ref[...]
            u = jax.nn.sigmoid(g[:, : 2 * LANES])
            uf[at, :] = u[:, :LANES]
            ub[at, :] = u[:, LANES:]
            cf[at, :] = g[:, 2 * LANES : 3 * LANES]
            cb[at, :] = g[:, 3 * LANES :]
    ones = jnp.ones((SEGS, LANES), F32)
    zeros = jnp.zeros((SEGS, LANES), F32)

    def at_step(step):
        return pl.ds(step, SEGS, stride=steps)

    def local(step, carry):
        h_f, p_f, h_b, p_b = carry
        at_f, at_b = at_step(step), at_step(steps - 1 - step)
        u = uf[at_f, :]
        a = 1.0 - u
        h_f = a * h_f + u * cf[at_f, :]
        p_f = a * p_f
        u = ub[at_b, :]
        a = 1.0 - u
        h_b = a * h_b + u * cb[at_b, :]
        p_b = a * p_b
        return h_f, p_f, h_b, p_b

    h_f, p_f, h_b, p_b = lax.fori_loop(0, steps, local, (zeros, ones, zeros, ones), unroll=4)
    hend[:, :LANES] = h_f
    hend[:, LANES:] = h_b
    pend[:, :LANES] = p_f
    pend[:, LANES:] = p_b
    one_f = jnp.zeros((1, LANES), F32)
    one_b = jnp.zeros((1, LANES), F32)
    for s in range(SEGS):
        r = SEGS - 1 - s
        hin[s : s + 1, :LANES] = one_f
        hin[r : r + 1, LANES:] = one_b
        one_f = pend[s : s + 1, :LANES] * one_f + hend[s : s + 1, :LANES]
        one_b = pend[r : r + 1, LANES:] * one_b + hend[r : r + 1, LANES:]

    def final(step, carry):
        h_f, h_b = carry
        at_f, at_b = at_step(step), at_step(steps - 1 - step)
        e = cf[at_f, :] - h_f
        cf[at_f, :] = e
        h_f = h_f + uf[at_f, :] * e
        hf[at_f, :] = h_f
        e = cb[at_b, :] - h_b
        cb[at_b, :] = e
        h_b = h_b + ub[at_b, :] * e
        hb[at_b, :] = h_b
        return h_f, h_b

    lax.fori_loop(0, steps, final, (hin[:, :LANES], hin[:, LANES:]), unroll=4)
    u_ref[0] = uf[...]
    u_ref[1] = ub[...]
    e_ref[0] = cf[...]
    e_ref[1] = cb[...]
    ends, starts = bounds_columns(len_ref, mask_ref, rows)
    iota = lax.broadcasted_iota(jnp.int32, (count, CHUNK), 1).astype(F32)
    acc_f = jnp.zeros((count, LANES), F32)
    acc_b = jnp.zeros((count, LANES), F32)
    for i in range(rows // CHUNK):
        pick = jnp.where(iota == ends - float(i * CHUNK), 1.0, 0.0).astype(BF16)
        acc_f = acc_f + dot_nn(pick, hf[i * CHUNK : (i + 1) * CHUNK, :].astype(BF16))
        pick = jnp.where(iota == starts - float(i * CHUNK), 1.0, 0.0).astype(BF16)
        acc_b = acc_b + dot_nn(pick, hb[i * CHUNK : (i + 1) * CHUNK, :].astype(BF16))
    pooled_ref[...] = jnp.concatenate([acc_f.astype(BF16), acc_b.astype(BF16)], axis=1)
    size = count // 4
    for k, (out, off) in enumerate(((part_b, 0), (part_b, size), (part_a, 0), (part_a, size))):
        pooled = pooled_ref[rows_at(me, k, size), :]
        out[off : off + size, :] = dot_nn(pooled, cw_ref[...]).astype(BF16)


def gru_forward(me, chr_blocks, w, b, lengths, mask, cw):
    rows, count = 4 * chr_blocks[0].shape[0], lengths.shape[1]
    outs = [
        ((2, rows, LANES), F32),
        ((2, rows, LANES), F32),
        ((count, 2 * LANES), BF16),
        ((count // 2, cw.shape[1]), BF16),
        ((count // 2, cw.shape[1]), BF16),
    ]
    scratch = [((rows, LANES), F32)] * 6 + [((SEGS, 2 * LANES), F32)] * 3
    flops = 2 * rows * CE * 4 * LANES * 8
    return full_call(
        gru_forward_kernel, outs, scratch, flops, me, *chr_blocks, w, b, lengths, mask, cw
    )


def gru_backward_kernel(
    me_ref, g0, g1, g2, g3, cw_ref, pooled_ref, u_ref, e_ref, c0, c1, c2, c3,
    w_ref, len_ref, mask_ref,
    gchr_a, gchr_b, gw_ref, gb_ref, gcw_ref,
    gmid, ef, eb, gf, gb, pend, hend, hin,
):
    me = me_ref[0]
    rows = 4 * c0.shape[0]
    count = len_ref.shape[1]
    steps = rows // SEGS
    for k, g_ref in enumerate((g0, g1, g2, g3)):
        gmid[rows_at(me, k, g0.shape[0]), :] = g_ref[...]
    gcw_ref[...] = dot_tn(pooled_ref[...], gmid[...]).astype(gcw_ref.dtype)
    g_pooled = dot_nt(gmid[...], cw_ref[...]).astype(BF16)
    row_i = lax.broadcasted_iota(jnp.int32, (count, count), 0)
    col_i = lax.broadcasted_iota(jnp.int32, (count, count), 1)
    upper = jnp.where(row_i <= col_i, 1.0, 0.0).astype(BF16)
    lens = len_ref[...].astype(F32)
    drop = mask_ref[...].astype(F32) * (-2.0 * rows)
    ends = dot_nn(lens.astype(BF16), upper) - 1.0
    starts = ends + 1.0 - lens + drop
    ends = ends + drop
    iota = lax.broadcasted_iota(jnp.int32, (CHUNK, count), 0).astype(F32)
    for i in range(rows // CHUNK):
        at = slice(i * CHUNK, (i + 1) * CHUNK)
        pick = jnp.where(iota == ends - float(i * CHUNK), 1.0, 0.0).astype(BF16)
        gf[at, :] = dot_nn(pick, g_pooled[:, :LANES])
        pick = jnp.where(iota == starts - float(i * CHUNK), 1.0, 0.0).astype(BF16)
        gb[at, :] = dot_nn(pick, g_pooled[:, LANES:])
    ones = jnp.ones((SEGS, LANES), F32)
    zeros = jnp.zeros((SEGS, LANES), F32)
    uf, ub = u_ref.at[0], u_ref.at[1]
    ef_in, eb_in = e_ref.at[0], e_ref.at[1]

    def at_step(step):
        return pl.ds(step, SEGS, stride=steps)

    def local(step, carry):
        x_f, p_f, x_b, p_b = carry
        at_f, at_b = at_step(steps - 1 - step), at_step(step)
        a = 1.0 - uf[at_f, :]
        x_f = a * (gf[at_f, :] + x_f)
        p_f = a * p_f
        a = 1.0 - ub[at_b, :]
        x_b = a * (gb[at_b, :] + x_b)
        p_b = a * p_b
        return x_f, p_f, x_b, p_b

    x_f, p_f, x_b, p_b = lax.fori_loop(0, steps, local, (zeros, ones, zeros, ones), unroll=4)
    hend[:, :LANES] = x_f
    hend[:, LANES:] = x_b
    pend[:, :LANES] = p_f
    pend[:, LANES:] = p_b
    one_f = jnp.zeros((1, LANES), F32)
    one_b = jnp.zeros((1, LANES), F32)
    for s in range(SEGS):
        r = SEGS - 1 - s
        hin[r : r + 1, :LANES] = one_f
        hin[s : s + 1, LANES:] = one_b
        one_f = pend[r : r + 1, :LANES] * one_f + hend[r : r + 1, :LANES]
        one_b = pend[s : s + 1, LANES:] * one_b + hend[s : s + 1, LANES:]

    def final(step, carry):
        x_f, x_b = carry
        at_f, at_b = at_step(steps - 1 - step), at_step(step)
        u = uf[at_f, :]
        d = gf[at_f, :] + x_f
        gf[at_f, :] = d * u
        x_f = (1.0 - u) * d
        ef[at_f, :] = ef_in[at_f, :] * (u * x_f)
        u = ub[at_b, :]
        d = gb[at_b, :] + x_b
        gb[at_b, :] = d * u
        x_b = (1.0 - u) * d
        eb[at_b, :] = eb_in[at_b, :] * (u * x_b)
        return x_f, x_b

    lax.fori_loop(0, steps, final, (hin[:, :LANES], hin[:, LANES:]), unroll=4)
    gw_acc = jnp.zeros(gw_ref.shape, F32)
    gb_acc = jnp.zeros((1, 4 * LANES), F32)
    size = c0.shape[0]
    for k, (c_ref, out, off) in enumerate(
        ((c0, gchr_b, 0), (c1, gchr_b, size), (c2, gchr_a, 0), (c3, gchr_a, size))
    ):
        for half in range(size // CHUNK):
            start = pl.multiple_of((me ^ ORDER[k]) * size + half * CHUNK, CHUNK)
            at = pl.ds(start, CHUNK)
            gates = jnp.concatenate(
                [ef[at, :], eb[at, :], gf[at, :], gb[at, :]], axis=1
            ).astype(BF16)
            gb_acc = gb_acc + jnp.sum(gates.astype(F32), axis=0, keepdims=True)
            own = slice(half * CHUNK, (half + 1) * CHUNK)
            out[off + half * CHUNK : off + (half + 1) * CHUNK, :] = dot_nt(
                gates, w_ref[...]
            ).astype(BF16)
            gw_acc = gw_acc + dot_tn(c_ref[own, :], gates)
    gw_ref[...] = gw_acc.astype(gw_ref.dtype)
    gb_ref[...] = gb_acc


def gru_backward(me, g_blocks, cw, pooled, u, e, chr_blocks, w, lengths, mask):
    size, count = chr_blocks[0].shape[0], lengths.shape[1]
    rows = 4 * size
    outs = [
        ((2 * size, CE), BF16),
        ((2 * size, CE), BF16),
        (w.shape, BF16),
        ((1, 4 * LANES), F32),
        (cw.shape, BF16),
    ]
    scratch = (
        [((count, cw.shape[1]), BF16)]
        + [((rows, LANES), F32)] * 4
        + [((SEGS, 2 * LANES), F32)] * 3
    )
    flops = 2 * rows * CE * 4 * LANES * 10
    return full_call(
        gru_backward_kernel, outs, scratch, flops,
        me, *g_blocks, cw, pooled, u, e, *chr_blocks, w, lengths, mask,
    )


def pick_kernel(me_ref, token_ref, char_ref, *outs):
    me = me_ref[0]
    width = outs[0].shape[1]
    for k, out in enumerate(outs):
        for c in range(4):
            @pl.when((me ^ ORDER[k]) == c)
            def _(out=out, c=c):
                source = token_ref if c < 2 else char_ref
                out[...] = source[:, (c % 2) * width : (c % 2 + 1) * width]


def column_blocks(me, token_rows, char_rows):
    rows, width = token_rows.shape
    outs = [((rows, width // 2), token_rows.dtype)] * 4
    return full_call(pick_kernel, outs, [], rows * width, me, token_rows, char_rows)


def place_kernel(me_ref, b0, b1, b2, b3, token_ref, char_ref):
    me = me_ref[0]
    width = b0.shape[1]
    for k, block in enumerate((b0, b1, b2, b3)):
        for c in range(4):
            @pl.when((me ^ ORDER[k]) == c)
            def _(block=block, c=c):
                target = token_ref if c < 2 else char_ref
                target[:, (c % 2) * width : (c % 2 + 1) * width] = block[...]


def from_columns(me, blocks):
    rows, width = blocks[0].shape
    outs = [((rows, 2 * width), blocks[0].dtype)] * 2
    return full_call(place_kernel, outs, [], rows * width, me, *blocks)


def row_sum(values):
    return jnp.sum(values, axis=1, keepdims=True)


def merge_forward_kernel(
    me_ref, s0, s1, s2, s3, m0, m1, m2, m3, k0, k1, k2, k3, w_ref, b_ref, tg_ref, cg_ref,
    joined_ref, v_ref, cot_ref, stat_ref, gain_vm,
):
    me = me_ref[0]
    size = s0.shape[0]
    rows, width = v_ref.shape
    for k, (s, m, c) in enumerate(zip((s0, s1, s2, s3), (m0, m1, m2, m3), (k0, k1, k2, k3))):
        at = rows_at(me, k, size)
        joined_ref[at, :D] = s[...]
        joined_ref[at, D:] = m[...]
        cot_ref[at, :] = c[...]
    row_i = lax.broadcasted_iota(jnp.int32, (rows, width), 0)
    joined = joined_ref[...]
    merged = dot_nn(joined, w_ref[1]) + b_ref[...]
    above = pltpu.roll(dot_nn(joined, w_ref[0]), 1, 0)
    merged = merged + jnp.where(row_i == 0, 0.0, above)
    below = pltpu.roll(dot_nn(joined, w_ref[2]), rows - 1, 0)
    merged = merged + jnp.where(row_i == rows - 1, 0.0, below)
    v_ref[...] = merged.astype(BF16).astype(F32)
    for c in range(4):
        @pl.when(me == c)
        def _(c=c):
            v_ref[...] += joined_ref[:, c * width : (c + 1) * width].astype(F32)
            gain = tg_ref if c < 2 else cg_ref
            gain_vm[...] = gain[:, (c % 2) * width : (c % 2 + 1) * width]
    v = v_ref[...]
    mean = row_sum(v) * (1.0 / width)
    centered = v - mean
    scaled = cot_ref[...].astype(F32) * gain_vm[...]
    lane = lax.broadcasted_iota(jnp.int32, (rows, LANES), 1)
    stats = jnp.where(lane == 0, mean, row_sum(centered * centered))
    stats = jnp.where(lane == 2, row_sum(scaled), stats)
    stat_ref[...] = jnp.where(lane == 3, row_sum(scaled * centered), stats)


def merge_forward(me, second, mid, cots, w, b, token_gain, char_gain):
    rows, width = 4 * second[0].shape[0], w.shape[2]
    outs = [
        ((rows, 2 * D), BF16),
        ((rows, width), F32),
        ((rows, width), BF16),
        ((rows, LANES), F32),
    ]
    return full_call(
        merge_forward_kernel, outs, [((1, width), F32)], 6 * rows * 2 * D * width,
        me, *second, *mid, *cots, w, b, token_gain, char_gain,
    )


def merge_backward_kernel(
    me_ref, v_ref, cot_ref, mine_ref, other_ref, w_ref, tg_ref, ts_ref, cg_ref, cs_ref,
    o0, o1, o2, o3, gcat_ref, part_a, part_b, sums_ref, gain_vm, shift_vm, out_vm, acc_vm,
):
    me = me_ref[0]
    rows, width = v_ref.shape
    size = rows // 4
    for c in range(4):
        @pl.when(me == c)
        def _(c=c):
            at = slice((c % 2) * width, (c % 2 + 1) * width)
            gain_vm[...] = (tg_ref if c < 2 else cg_ref)[:, at]
            shift_vm[...] = (ts_ref if c < 2 else cs_ref)[:, at]
    mine, other = mine_ref[...], other_ref[...]
    mean_m, mean_o = mine[:, 0:1], other[:, 0:1]
    mean = 0.5 * (mean_m + mean_o)
    gap = mean_m - mean_o
    spread = mine[:, 1:2] + other[:, 1:2] + (0.5 * width) * gap * gap
    inverse = 0.5 / width
    r = lax.rsqrt(spread * inverse + epsilon)
    mean_cg = (mine[:, 2:3] + other[:, 2:3]) * inverse
    cross = (
        mine[:, 3:4] + (mean_m - mean) * mine[:, 2:3] + other[:, 3:4] + (mean_o - mean) * other[:, 2:3]
    )
    mean_cgx = cross * inverse * r
    gain = gain_vm[...]
    cot = cot_ref[...].astype(F32)
    xhat = (v_ref[...] - mean) * r
    out_vm[...] = (xhat * gain + shift_vm[...]).astype(BF16)
    for k, out in enumerate((o0, o1, o2, o3)):
        out[...] = out_vm[rows_at(me, k, size), :]
    g = r * (cot * gain - mean_cg - xhat * mean_cgx)
    g_low = g.astype(BF16)
    g_wide = g_low.astype(F32)
    row_i = lax.broadcasted_iota(jnp.int32, (rows, width), 0)
    after = jnp.where(row_i == rows - 1, 0.0, pltpu.roll(g_wide, rows - 1, 0)).astype(BF16)
    before = jnp.where(row_i == 0, 0.0, pltpu.roll(g_wide, 1, 0)).astype(BF16)
    gcat_ref[0] = after
    gcat_ref[1] = g_low
    gcat_ref[2] = before
    sums_ref[...] = jnp.zeros(sums_ref.shape, F32)
    sums_ref[0:1, :] = jnp.sum(cot * xhat, axis=0, keepdims=True)
    sums_ref[1:2, :] = jnp.sum(cot, axis=0, keepdims=True)
    sums_ref[2:3, :] = jnp.sum(g_wide, axis=0, keepdims=True)
    acc_vm[...] = dot_nt(after, w_ref[0]) + dot_nt(g_low, w_ref[1]) + dot_nt(before, w_ref[2])
    for c in range(4):
        @pl.when(me == c)
        def _(c=c):
            acc_vm[:, c * width : (c + 1) * width] += g
    for k, (out, off) in enumerate(((part_b, 0), (part_b, size), (part_a, 0), (part_a, size))):
        out[off : off + size, :] = acc_vm[rows_at(me, k, size), :].astype(BF16)


def merge_backward(me, v, cot, mine, other, w, norms):
    rows, width = v.shape
    outs = (
        [((rows // 4, width), BF16)] * 4
        + [((3, rows, width), BF16)]
        + [((rows // 2, 2 * D), BF16)] * 2
        + [((8, width), F32)]
    )
    scratch = [((1, width), F32)] * 2 + [((rows, width), BF16), ((rows, 2 * D), F32)]
    return full_call(
        merge_backward_kernel, outs, scratch, 6 * rows * 2 * D * width,
        me, v, cot, mine, other, w, *norms,
    )


def merge_weight_kernel(joined_ref, gcat_ref, out_ref):
    joined_t = joined_ref[...].T
    for o in range(3):
        out_ref[o] = dot_nn(joined_t, gcat_ref[o]).astype(BF16)


def merge_weight_grad(joined, gcat):
    rows, width = gcat.shape[1:]
    outs = [((3, joined.shape[1], width), BF16)]
    return full_call(
        merge_weight_kernel, outs, [], 6 * rows * joined.shape[1] * width, joined, gcat
    )[0]


def layer_norm(values, gain_vec, shift_vec):
    row_mean = jnp.mean(values, axis=-1, keepdims=True)
    centered = values - row_mean
    row_var = jnp.mean(centered * centered, axis=-1, keepdims=True)
    return centered * lax.rsqrt(row_var + epsilon) * gain_vec + shift_vec


def gelu_exact(values):
    return jax.nn.gelu(values, approximate=False)


def rounded(values):
    return values.astype(jnp.bfloat16)


def wide(values):
    return values.astype(jnp.float32)


def pad_units(array, axis):
    pads = [(0, 0)] * array.ndim
    pads[axis] = (0, LANES - array.shape[axis])
    return jnp.pad(array, pads)


def swap(array, axis, bit, size):
    return lax.ppermute(array, axis, [(i, i ^ bit) for i in range(size)])


def across(array, bit):
    return swap(array, "tensor", bit, 4)


def gather(own):
    far = across(own, 2)
    near = across(own, 1)
    return [own, far, near, across(far, 1)]


def scatter(part_a, part_b):
    size = part_b.shape[0] // 2
    near = across(part_a, 1)
    passed = rounded(wide(part_b[size:]) + wide(near[size:]))
    far = across(passed, 2)
    return wide(part_b[:size]) + wide(near[:size]) + wide(far)


def halves(part):
    low = rounded(part)
    count = low.shape[0] // 2
    return low[count:], low[:count]


def make_body(dp_size):
    def total_small(values):
        bit = 1
        while bit < dp_size:
            values = values + swap(values, "dp", bit, dp_size)
            bit *= 2
        return values

    def total_weights(*parts):
        return [wide(total) for total in lax.psum(tuple(rounded(part) for part in parts), "dp")]

    def body(
        tokens,
        chars,
        lengths,
        mask,
        qkv_weight,
        qkv_bias,
        out_weight,
        out_bias,
        attn_gain,
        attn_shift,
        ffn_in_weight,
        ffn_in_bias,
        ffn_out_weight,
        ffn_out_bias,
        ffn_gain,
        ffn_shift,
        gru_weight,
        gate_bias,
        cand_bias,
        char_weight,
        char_bias,
        merge_weight,
        merge_bias,
        token_gain,
        token_shift,
        char_gain,
        char_shift,
        token_cot,
        char_cot,
    ):
        place = lax.axis_index("tensor")
        me = place.astype(jnp.int32).reshape(1)
        head_count = qkv_weight.shape[2]
        unit_count = gru_weight.shape[3]
        tok_all = jnp.concatenate(gather(tokens))
        chr_blocks = gather(chars)
        seq_rows = tok_all.shape[0]
        cot_parts = column_blocks(me, token_cot, char_cot)
        cot_blocks = [cot_parts[0]] + [across(cot_parts[k], ORDER[k]) for k in range(1, 4)]
        projected = jnp.dot(
            tok_all, qkv_weight.reshape(D, -1), preferred_element_type=jnp.float32
        ).reshape(seq_rows, 3, head_count, HD)
        queries = rounded((projected[:, 0] + qkv_bias[0]) * 0.125)
        key_rows = rounded(projected[:, 1])
        values = rounded(projected[:, 2] + qkv_bias[1])
        scores = jnp.einsum("qhd,khd->hqk", queries, key_rows, preferred_element_type=jnp.float32)
        maxima = jnp.max(scores, axis=-1, keepdims=True)
        totals = jnp.sum(jnp.exp(scores - maxima), axis=-1, keepdims=True)
        log_norm = maxima + jnp.log(totals)
        probs_low = rounded(jnp.exp(scores - log_norm))
        mixed = rounded(
            jnp.einsum("hqk,khd->qhd", probs_low, values, preferred_element_type=jnp.float32)
        ).reshape(seq_rows, head_count * HD)
        attn_part = jnp.dot(mixed, out_weight.reshape(-1, D), preferred_element_type=jnp.float32)
        wide_gru = pad_units(gru_weight, 3).reshape(CE, -1)
        wide_bias = pad_units(jnp.stack([gate_bias, cand_bias]), 2).reshape(1, -1)
        wide_char = pad_units(char_weight, 1).reshape(-1, D)
        update, excess, pooled_low, char_a, char_b = gru_forward(
            me, chr_blocks, wide_gru, wide_bias, lengths, mask, wide_char
        )
        first_in = wide(tokens) + scatter(*halves(attn_part)) + out_bias
        first_out, first_pull = jax.vjp(layer_norm, first_in, attn_gain, attn_shift)
        first_low_all = jnp.concatenate(gather(rounded(first_out)))
        hidden_pre = (
            jnp.dot(first_low_all, ffn_in_weight, preferred_element_type=jnp.float32) + ffn_in_bias
        )
        inter_full, gelu_pull = jax.vjp(gelu_exact, hidden_pre)
        inter_low = rounded(inter_full)
        ffn_part = jnp.dot(inter_low, ffn_out_weight, preferred_element_type=jnp.float32)
        char_mid = scatter(char_a, char_b) + char_bias
        mid_blocks = gather(rounded(char_mid))
        ffn_sum = scatter(*halves(ffn_part))
        second_out, second_pull = jax.vjp(
            layer_norm, first_out + ffn_sum + ffn_out_bias, ffn_gain, ffn_shift
        )
        second_blocks = gather(rounded(second_out))
        norms = [vec.reshape(1, -1) for vec in (token_gain, token_shift, char_gain, char_shift)]
        joined, mixed_cols, cot_cols, stats = merge_forward(
            me, second_blocks, mid_blocks, cot_blocks, merge_weight, merge_bias.reshape(1, -1),
            norms[0], norms[2],
        )
        other_stats = across(stats, 1)
        *out_parts, g_cat, joint_a, joint_b, merge_sums = merge_backward(
            me, mixed_cols, cot_cols, stats, other_stats, merge_weight, norms
        )
        out_blocks = [out_parts[0]] + [across(out_parts[k], ORDER[k]) for k in range(1, 4)]
        token_out, char_out = from_columns(me, out_blocks)
        g_rows = scatter(joint_a, joint_b)
        grad_merge_weight = merge_weight_grad(joined, g_cat)
        g_mid_low = rounded(g_rows[:, D:])
        ffn_in_grad, grad_ffn_gain, grad_ffn_shift = second_pull(g_rows[:, :D])
        ffn_grad_low = rounded(ffn_in_grad)
        grad_ffn_out_bias = jnp.sum(wide(ffn_grad_low), axis=0)
        grad_char_bias = jnp.sum(wide(g_mid_low), axis=0)
        ffn_grad_all = jnp.concatenate(gather(ffn_grad_low))
        g_mid_blocks = gather(g_mid_low)
        inter_grad = jnp.einsum(
            "td,fd->tf", ffn_grad_all, ffn_out_weight, preferred_element_type=jnp.float32
        )
        hidden_grad = rounded(gelu_pull(inter_grad)[0])
        first_part = jnp.einsum(
            "tf,cf->tc", hidden_grad, ffn_in_weight, preferred_element_type=jnp.float32
        )
        first_rows = scatter(*halves(first_part))
        grad_ffn_in_bias = jnp.sum(wide(hidden_grad), axis=0)
        grad_ffn_in_weight = jnp.einsum(
            "tc,tf->cf", first_low_all, hidden_grad, preferred_element_type=jnp.float32
        )
        grad_ffn_out_weight = jnp.einsum(
            "tf,td->fd", inter_low, ffn_grad_all, preferred_element_type=jnp.float32
        )
        g_chr_a, g_chr_b, wide_gru_grad, wide_bias_grad, wide_char_grad = gru_backward(
            me, g_mid_blocks, wide_char, pooled_low, update, excess, chr_blocks, wide_gru,
            lengths, mask,
        )
        chars_grad = rounded(scatter(g_chr_a, g_chr_b))
        grad_gru_weight = wide_gru_grad.reshape(CE, 2, 2, LANES)[..., :unit_count]
        wide_bias_grad = wide_bias_grad.reshape(2, 2, LANES)[..., :unit_count]
        grad_char_weight = wide_char_grad.reshape(2, LANES, D)[:, :unit_count]
        g_resid, grad_attn_gain, grad_attn_shift = first_pull(ffn_in_grad + first_rows)
        g_attn_low = rounded(g_resid)
        grad_out_bias = jnp.sum(wide(g_attn_low), axis=0)
        g_attn_all = jnp.concatenate(gather(g_attn_low))
        grad_out_weight = jnp.einsum(
            "tk,td->kd", mixed, g_attn_all, preferred_element_type=jnp.float32
        ).reshape(out_weight.shape)
        g_mixed = rounded(
            jnp.einsum(
                "td,kd->tk", g_attn_all, out_weight.reshape(-1, D),
                preferred_element_type=jnp.float32,
            )
        ).reshape(seq_rows, head_count, HD)
        scores_again = jnp.einsum(
            "qhd,khd->hqk", queries, key_rows, preferred_element_type=jnp.float32
        )
        probs_again = jnp.exp(scores_again - log_norm)
        probs_again_low = rounded(probs_again)
        g_values = jnp.einsum(
            "hqk,qhd->khd", probs_again_low, g_mixed, preferred_element_type=jnp.float32
        )
        g_probs = jnp.einsum("qhd,khd->hqk", g_mixed, values, preferred_element_type=jnp.float32)
        g_scores = rounded(
            probs_again * (g_probs - jnp.sum(g_probs * probs_again, axis=-1, keepdims=True))
        )
        g_queries = jnp.einsum(
            "hqk,khd->qhd", g_scores, key_rows, preferred_element_type=jnp.float32
        )
        g_keys = jnp.einsum("hqk,qhd->khd", g_scores, queries, preferred_element_type=jnp.float32)
        g_project = jnp.stack(
            [rounded(g_queries) * 0.125, rounded(g_keys), rounded(g_values)], axis=1
        )
        g_flat = g_project.reshape(seq_rows, -1)
        grad_qkv_weight = jnp.einsum(
            "tc,tf->cf", tok_all, g_flat, preferred_element_type=jnp.float32
        ).reshape(qkv_weight.shape)
        grad_qkv_bias = jnp.stack(
            [jnp.sum(wide(g_project[:, 0]), axis=0), jnp.sum(wide(g_project[:, 2]), axis=0)]
        )
        g_tok_all = jnp.einsum(
            "tf,cf->tc", g_flat, qkv_weight.reshape(D, -1), preferred_element_type=jnp.float32
        )
        token_grad = rounded(g_resid + scatter(*halves(g_tok_all)))
        width = merge_sums.shape[1]
        col_grads = lax.dynamic_update_slice(
            jnp.zeros((2, 4 * width), jnp.float32), merge_sums[0:2], (0, place * width)
        ).reshape(4, D)
        row_grads = jnp.stack(
            [
                grad_out_bias,
                grad_attn_gain,
                grad_attn_shift,
                grad_ffn_out_bias,
                grad_ffn_gain,
                grad_ffn_shift,
                grad_char_bias,
            ]
        )
        norm_parts = jnp.concatenate([row_grads, col_grads])
        norm_parts = norm_parts + across(norm_parts, 1)
        norm_parts = norm_parts + across(norm_parts, 2)
        norm_rows = lax.dynamic_slice_in_dim(norm_parts, place * (D // 4), D // 4, 1)
        smalls = [
            norm_rows,
            wide_bias_grad,
            merge_sums[2],
            grad_ffn_in_bias,
        ]
        flat = jnp.concatenate([small.reshape(-1) for small in smalls])
        flat = total_small(flat)
        totals = []
        start = 0
        for small in smalls:
            totals.append(flat[start : start + small.size].reshape(small.shape))
            start += small.size
        norm_rows, gate_grads, grad_merge_bias, grad_ffn_in_bias = totals
        grad_qkv_bias = total_small(grad_qkv_bias)
        (grad_merge_weight,) = total_weights(grad_merge_weight)
        (
            grad_qkv_weight,
            grad_out_weight,
            grad_gru_weight,
            grad_char_weight,
            grad_ffn_in_weight,
            grad_ffn_out_weight,
        ) = total_weights(
            grad_qkv_weight,
            grad_out_weight,
            grad_gru_weight,
            grad_char_weight,
            grad_ffn_in_weight,
            grad_ffn_out_weight,
        )
        return (
            token_out,
            char_out,
            token_grad,
            chars_grad,
            grad_qkv_weight,
            grad_qkv_bias,
            grad_out_weight,
            norm_rows[0],
            norm_rows[1],
            norm_rows[2],
            grad_ffn_in_weight,
            grad_ffn_in_bias,
            grad_ffn_out_weight,
            norm_rows[3],
            norm_rows[4],
            norm_rows[5],
            grad_gru_weight,
            gate_grads[0],
            gate_grads[1],
            grad_char_weight,
            norm_rows[6],
            grad_merge_weight,
            grad_merge_bias,
            norm_rows[7],
            norm_rows[9],
            norm_rows[8],
            norm_rows[10],
        )

    return body


def solution(mesh):
    in_specs = (
        P(("dp", "tensor"), None),
        P(("dp", "tensor"), None),
        P("dp", None),
        P("dp", None),
        P(None, None, "tensor", None),
        P(None, "tensor", None),
        P("tensor", None, None),
        P(),
        P(),
        P(),
        P(None, "tensor"),
        P("tensor"),
        P("tensor", None),
        P(),
        P(),
        P(),
        P(None, None, None, "tensor"),
        P(None, "tensor"),
        P(None, "tensor"),
        P(None, "tensor", None),
        P(),
        P(None, None, "tensor"),
        P("tensor"),
        P(),
        P(),
        P(),
        P(),
        P(("dp", "tensor"), None),
        P(("dp", "tensor"), None),
    )
    out_specs = (
        P(("dp", "tensor"), None),
        P(("dp", "tensor"), None),
        P(("dp", "tensor"), None),
        P(("dp", "tensor"), None),
        P(None, None, "tensor", None),
        P(None, "tensor", None),
        P("tensor", None, None),
        P("tensor"),
        P("tensor"),
        P("tensor"),
        P(None, "tensor"),
        P("tensor"),
        P("tensor", None),
        P("tensor"),
        P("tensor"),
        P("tensor"),
        P(None, None, None, "tensor"),
        P(None, "tensor"),
        P(None, "tensor"),
        P(None, "tensor", None),
        P("tensor"),
        P(None, None, "tensor"),
        P("tensor"),
        P("tensor"),
        P("tensor"),
        P("tensor"),
        P("tensor"),
    )
    return jax.shard_map(
        make_body(mesh.shape["dp"]), mesh=mesh, in_specs=in_specs, out_specs=out_specs, check_vma=False)
```

```python
import math

import jax
import jax.numpy as jnp
from jax import lax
from jax.experimental import pallas as pl
from jax.experimental.pallas import tpu as pltpu
from jax.sharding import PartitionSpec as P

D = 768
HD = 64
CE = 256
epsilon = 1e-05
F32 = jnp.float32
BF16 = jnp.bfloat16
LANES = 128
SEGS = 32
CHUNK = 256
ORDER = (0, 2, 1, 3)


def full_call(kernel, outs, scratch, flops, *args):
    vmem = pl.BlockSpec(memory_space=pltpu.VMEM)
    smem = pl.BlockSpec(memory_space=pltpu.SMEM)
    return pl.pallas_call(
        kernel,
        out_shape=[jax.ShapeDtypeStruct(shape, kind) for shape, kind in outs],
        in_specs=[smem if a.shape == (1,) else vmem for a in args],
        out_specs=[vmem] * len(outs),
        scratch_shapes=[pltpu.VMEM(shape, kind) for shape, kind in scratch],
        cost_estimate=pl.CostEstimate(
            flops=int(flops),
            transcendentals=0,
            bytes_accessed=sum(a.size * a.dtype.itemsize for a in args)
            + sum(jnp.dtype(kind).itemsize * math.prod(shape) for shape, kind in outs),
        ),
    )(*args)


def dot_nn(a, b):
    return lax.dot_general(a, b, (((1,), (0,)), ((), ())), preferred_element_type=F32)


def dot_nt(a, b):
    return lax.dot_general(a, b, (((1,), (1,)), ((), ())), preferred_element_type=F32)


def dot_tn(a, b):
    return lax.dot_general(a, b, (((0,), (0,)), ((), ())), preferred_element_type=F32)


def rows_at(me, k, size):
    return pl.ds(pl.multiple_of((me ^ ORDER[k]) * size, size), size)


def bounds_columns(len_ref, mask_ref, rows):
    count = len_ref.shape[1]
    row_i = lax.broadcasted_iota(jnp.int32, (count, count), 0)
    col_i = lax.broadcasted_iota(jnp.int32, (count, count), 1)
    lens = len_ref[...].astype(F32)
    drop = mask_ref[...].astype(F32) * (-2.0 * rows)
    own = jnp.where(row_i == col_i, drop, 0.0)
    ends = jnp.sum(jnp.where(col_i <= row_i, lens, 0.0) + own, axis=1, keepdims=True) - 1.0
    starts = jnp.sum(jnp.where(col_i < row_i, lens, 0.0) + own, axis=1, keepdims=True)
    return ends, starts


def gru_forward_kernel(
    me_ref, c0, c1, c2, c3, w_ref, b_ref, len_ref, mask_ref, cw_ref,
    u_ref, e_ref, pooled_ref, part_a, part_b,
    uf, ub, cf, cb, hf, hb, pend, hend, hin,
):
    me = me_ref[0]
    rows = 4 * c0.shape[0]
    count = len_ref.shape[1]
    steps = rows // SEGS
    for k, c_ref in enumerate((c0, c1, c2, c3)):
        for half in range(c0.shape[0] // CHUNK):
            start = pl.multiple_of((me ^ ORDER[k]) * c0.shape[0] + half * CHUNK, CHUNK)
            at = pl.ds(start, CHUNK)
            g = dot_nn(c_ref[half * CHUNK : (half + 1) * CHUNK, :], w_ref[...]) + b_ref[...]
            u = jax.nn.sigmoid(g[:, : 2 * LANES])
            uf[at, :] = u[:, :LANES]
            ub[at, :] = u[:, LANES:]
            cf[at, :] = g[:, 2 * LANES : 3 * LANES]
            cb[at, :] = g[:, 3 * LANES :]
    ones = jnp.ones((SEGS, LANES), F32)
    zeros = jnp.zeros((SEGS, LANES), F32)

    def at_step(step):
        return pl.ds(step, SEGS, stride=steps)

    def local(step, carry):
        h_f, p_f, h_b, p_b = carry
        at_f, at_b = at_step(step), at_step(steps - 1 - step)
        u = uf[at_f, :]
        a = 1.0 - u
        h_f = a * h_f + u * cf[at_f, :]
        p_f = a * p_f
        u = ub[at_b, :]
        a = 1.0 - u
        h_b = a * h_b + u * cb[at_b, :]
        p_b = a * p_b
        return h_f, p_f, h_b, p_b

    h_f, p_f, h_b, p_b = lax.fori_loop(0, steps, local, (zeros, ones, zeros, ones), unroll=4)
    hend[:, :LANES] = h_f
    hend[:, LANES:] = h_b
    pend[:, :LANES] = p_f
    pend[:, LANES:] = p_b
    one_f = jnp.zeros((1, LANES), F32)
    one_b = jnp.zeros((1, LANES), F32)
    for s in range(SEGS):
        r = SEGS - 1 - s
        hin[s : s + 1, :LANES] = one_f
        hin[r : r + 1, LANES:] = one_b
        one_f = pend[s : s + 1, :LANES] * one_f + hend[s : s + 1, :LANES]
        one_b = pend[r : r + 1, LANES:] * one_b + hend[r : r + 1, LANES:]

    def final(step, carry):
        h_f, h_b = carry
        at_f, at_b = at_step(step), at_step(steps - 1 - step)
        e = cf[at_f, :] - h_f
        cf[at_f, :] = e
        h_f = h_f + uf[at_f, :] * e
        hf[at_f, :] = h_f
        e = cb[at_b, :] - h_b
        cb[at_b, :] = e
        h_b = h_b + ub[at_b, :] * e
        hb[at_b, :] = h_b
        return h_f, h_b

    lax.fori_loop(0, steps, final, (hin[:, :LANES], hin[:, LANES:]), unroll=4)
    u_ref[0] = uf[...]
    u_ref[1] = ub[...]
    e_ref[0] = cf[...]
    e_ref[1] = cb[...]
    ends, starts = bounds_columns(len_ref, mask_ref, rows)
    iota = lax.broadcasted_iota(jnp.int32, (count, CHUNK), 1).astype(F32)
    acc_f = jnp.zeros((count, LANES), F32)
    acc_b = jnp.zeros((count, LANES), F32)
    for i in range(rows // CHUNK):
        pick = jnp.where(iota == ends - float(i * CHUNK), 1.0, 0.0).astype(BF16)
        acc_f = acc_f + dot_nn(pick, hf[i * CHUNK : (i + 1) * CHUNK, :].astype(BF16))
        pick = jnp.where(iota == starts - float(i * CHUNK), 1.0, 0.0).astype(BF16)
        acc_b = acc_b + dot_nn(pick, hb[i * CHUNK : (i + 1) * CHUNK, :].astype(BF16))
    pooled_ref[...] = jnp.concatenate([acc_f.astype(BF16), acc_b.astype(BF16)], axis=1)
    size = count // 4
    for k, (out, off) in enumerate(((part_b, 0), (part_b, size), (part_a, 0), (part_a, size))):
        pooled = pooled_ref[rows_at(me, k, size), :]
        out[off : off + size, :] = dot_nn(pooled, cw_ref[...]).astype(BF16)


def gru_forward(me, chr_blocks, w, b, lengths, mask, cw):
    rows, count = 4 * chr_blocks[0].shape[0], lengths.shape[1]
    outs = [
        ((2, rows, LANES), F32),
        ((2, rows, LANES), F32),
        ((count, 2 * LANES), BF16),
        ((count // 2, cw.shape[1]), BF16),
        ((count // 2, cw.shape[1]), BF16),
    ]
    scratch = [((rows, LANES), F32)] * 6 + [((SEGS, 2 * LANES), F32)] * 3
    flops = 2 * rows * CE * 4 * LANES * 8
    return full_call(
        gru_forward_kernel, outs, scratch, flops, me, *chr_blocks, w, b, lengths, mask, cw
    )


def gru_backward_kernel(
    me_ref, g0, g1, g2, g3, cw_ref, pooled_ref, u_ref, e_ref, c0, c1, c2, c3,
    w_ref, len_ref, mask_ref,
    gchr_a, gchr_b, gw_ref, gb_ref, gcw_ref,
    gmid, ef, eb, gf, gb, pend, hend, hin,
):
    me = me_ref[0]
    rows = 4 * c0.shape[0]
    count = len_ref.shape[1]
    steps = rows // SEGS
    for k, g_ref in enumerate((g0, g1, g2, g3)):
        gmid[rows_at(me, k, g0.shape[0]), :] = g_ref[...]
    gcw_ref[...] = dot_tn(pooled_ref[...], gmid[...]).astype(gcw_ref.dtype)
    g_pooled = dot_nt(gmid[...], cw_ref[...]).astype(BF16)
    row_i = lax.broadcasted_iota(jnp.int32, (count, count), 0)
    col_i = lax.broadcasted_iota(jnp.int32, (count, count), 1)
    upper = jnp.where(row_i <= col_i, 1.0, 0.0).astype(BF16)
    lens = len_ref[...].astype(F32)
    drop = mask_ref[...].astype(F32) * (-2.0 * rows)
    ends = dot_nn(lens.astype(BF16), upper) - 1.0
    starts = ends + 1.0 - lens + drop
    ends = ends + drop
    iota = lax.broadcasted_iota(jnp.int32, (CHUNK, count), 0).astype(F32)
    for i in range(rows // CHUNK):
        at = slice(i * CHUNK, (i + 1) * CHUNK)
        pick = jnp.where(iota == ends - float(i * CHUNK), 1.0, 0.0).astype(BF16)
        gf[at, :] = dot_nn(pick, g_pooled[:, :LANES])
        pick = jnp.where(iota == starts - float(i * CHUNK), 1.0, 0.0).astype(BF16)
        gb[at, :] = dot_nn(pick, g_pooled[:, LANES:])
    ones = jnp.ones((SEGS, LANES), F32)
    zeros = jnp.zeros((SEGS, LANES), F32)
    uf, ub = u_ref.at[0], u_ref.at[1]
    ef_in, eb_in = e_ref.at[0], e_ref.at[1]

    def at_step(step):
        return pl.ds(step, SEGS, stride=steps)

    def local(step, carry):
        x_f, p_f, x_b, p_b = carry
        at_f, at_b = at_step(steps - 1 - step), at_step(step)
        a = 1.0 - uf[at_f, :]
        x_f = a * (gf[at_f, :] + x_f)
        p_f = a * p_f
        a = 1.0 - ub[at_b, :]
        x_b = a * (gb[at_b, :] + x_b)
        p_b = a * p_b
        return x_f, p_f, x_b, p_b

    x_f, p_f, x_b, p_b = lax.fori_loop(0, steps, local, (zeros, ones, zeros, ones), unroll=4)
    hend[:, :LANES] = x_f
    hend[:, LANES:] = x_b
    pend[:, :LANES] = p_f
    pend[:, LANES:] = p_b
    one_f = jnp.zeros((1, LANES), F32)
    one_b = jnp.zeros((1, LANES), F32)
    for s in range(SEGS):
        r = SEGS - 1 - s
        hin[r : r + 1, :LANES] = one_f
        hin[s : s + 1, LANES:] = one_b
        one_f = pend[r : r + 1, :LANES] * one_f + hend[r : r + 1, :LANES]
        one_b = pend[s : s + 1, LANES:] * one_b + hend[s : s + 1, LANES:]

    def final(step, carry):
        x_f, x_b = carry
        at_f, at_b = at_step(steps - 1 - step), at_step(step)
        u = uf[at_f, :]
        d = gf[at_f, :] + x_f
        gf[at_f, :] = d * u
        x_f = (1.0 - u) * d
        ef[at_f, :] = ef_in[at_f, :] * (u * x_f)
        u = ub[at_b, :]
        d = gb[at_b, :] + x_b
        gb[at_b, :] = d * u
        x_b = (1.0 - u) * d
        eb[at_b, :] = eb_in[at_b, :] * (u * x_b)
        return x_f, x_b

    lax.fori_loop(0, steps, final, (hin[:, :LANES], hin[:, LANES:]), unroll=4)
    gw_acc = jnp.zeros(gw_ref.shape, F32)
    gb_acc = jnp.zeros((1, 4 * LANES), F32)
    size = c0.shape[0]
    for k, (c_ref, out, off) in enumerate(
        ((c0, gchr_b, 0), (c1, gchr_b, size), (c2, gchr_a, 0), (c3, gchr_a, size))
    ):
        for half in range(size // CHUNK):
            start = pl.multiple_of((me ^ ORDER[k]) * size + half * CHUNK, CHUNK)
            at = pl.ds(start, CHUNK)
            gates = jnp.concatenate(
                [ef[at, :], eb[at, :], gf[at, :], gb[at, :]], axis=1
            ).astype(BF16)
            gb_acc = gb_acc + jnp.sum(gates.astype(F32), axis=0, keepdims=True)
            own = slice(half * CHUNK, (half + 1) * CHUNK)
            out[off + half * CHUNK : off + (half + 1) * CHUNK, :] = dot_nt(
                gates, w_ref[...]
            ).astype(BF16)
            gw_acc = gw_acc + dot_tn(c_ref[own, :], gates)
    gw_ref[...] = gw_acc.astype(gw_ref.dtype)
    gb_ref[...] = gb_acc


def gru_backward(me, g_blocks, cw, pooled, u, e, chr_blocks, w, lengths, mask):
    size, count = chr_blocks[0].shape[0], lengths.shape[1]
    rows = 4 * size
    outs = [
        ((2 * size, CE), BF16),
        ((2 * size, CE), BF16),
        (w.shape, BF16),
        ((1, 4 * LANES), F32),
        (cw.shape, BF16),
    ]
    scratch = (
        [((count, cw.shape[1]), BF16)]
        + [((rows, LANES), F32)] * 4
        + [((SEGS, 2 * LANES), F32)] * 3
    )
    flops = 2 * rows * CE * 4 * LANES * 10
    return full_call(
        gru_backward_kernel, outs, scratch, flops,
        me, *g_blocks, cw, pooled, u, e, *chr_blocks, w, lengths, mask,
    )


def pick_kernel(me_ref, token_ref, char_ref, *outs):
    me = me_ref[0]
    width = outs[0].shape[1]
    for k, out in enumerate(outs):
        for c in range(4):
            @pl.when((me ^ ORDER[k]) == c)
            def _(out=out, c=c):
                source = token_ref if c < 2 else char_ref
                out[...] = source[:, (c % 2) * width : (c % 2 + 1) * width]


def column_blocks(me, token_rows, char_rows):
    rows, width = token_rows.shape
    outs = [((rows, width // 2), token_rows.dtype)] * 4
    return full_call(pick_kernel, outs, [], rows * width, me, token_rows, char_rows)


def place_kernel(me_ref, b0, b1, b2, b3, token_ref, char_ref):
    me = me_ref[0]
    width = b0.shape[1]
    for k, block in enumerate((b0, b1, b2, b3)):
        for c in range(4):
            @pl.when((me ^ ORDER[k]) == c)
            def _(block=block, c=c):
                target = token_ref if c < 2 else char_ref
                target[:, (c % 2) * width : (c % 2 + 1) * width] = block[...]


def from_columns(me, blocks):
    rows, width = blocks[0].shape
    outs = [((rows, 2 * width), blocks[0].dtype)] * 2
    return full_call(place_kernel, outs, [], rows * width, me, *blocks)


def row_sum(values):
    return jnp.sum(values, axis=1, keepdims=True)


def merge_forward_kernel(
    me_ref, s0, s1, s2, s3, m0, m1, m2, m3, k0, k1, k2, k3, w_ref, b_ref, vec_ref,
    joined_ref, v_ref, cot_ref, stat_ref, gain_vm,
):
    me = me_ref[0]
    size = s0.shape[0]
    rows, width = v_ref.shape
    for k, (s, m, c) in enumerate(zip((s0, s1, s2, s3), (m0, m1, m2, m3), (k0, k1, k2, k3))):
        at = rows_at(me, k, size)
        joined_ref[at, :D] = s[...]
        joined_ref[at, D:] = m[...]
        cot_ref[at, :] = c[...]
    row_i = lax.broadcasted_iota(jnp.int32, (rows, width), 0)
    joined = joined_ref[...]
    merged = dot_nn(joined, w_ref[1]) + b_ref[...]
    above = pltpu.roll(dot_nn(joined, w_ref[0]), 1, 0)
    merged = merged + jnp.where(row_i == 0, 0.0, above)
    below = pltpu.roll(dot_nn(joined, w_ref[2]), rows - 1, 0)
    merged = merged + jnp.where(row_i == rows - 1, 0.0, below)
    v_ref[...] = merged.astype(BF16).astype(F32)
    for c in range(4):
        @pl.when(me == c)
        def _(c=c):
            v_ref[...] += joined_ref[:, c * width : (c + 1) * width].astype(F32)
            at = slice((c % 2) * width, (c % 2 + 1) * width)
            gain_vm[...] = vec_ref[c // 2 : c // 2 + 1, at]
    v = v_ref[...]
    mean = row_sum(v) * (1.0 / width)
    centered = v - mean
    scaled = cot_ref[...].astype(F32) * gain_vm[...]
    lane = lax.broadcasted_iota(jnp.int32, (rows, LANES), 1)
    stats = jnp.where(lane == 0, mean, row_sum(centered * centered))
    stats = jnp.where(lane == 2, row_sum(scaled), stats)
    stat_ref[...] = jnp.where(lane == 3, row_sum(scaled * centered), stats)


def merge_forward(me, second, mid, cots, w, b, vecs):
    rows, width = 4 * second[0].shape[0], w.shape[2]
    outs = [
        ((rows, 2 * D), BF16),
        ((rows, width), F32),
        ((rows, width), BF16),
        ((rows, LANES), F32),
    ]
    return full_call(
        merge_forward_kernel, outs, [((1, width), F32)], 6 * rows * 2 * D * width,
        me, *second, *mid, *cots, w, b, vecs,
    )


def merge_backward_kernel(
    me_ref, v_ref, cot_ref, mine_ref, other_ref, w_ref, vec_ref,
    o0, o1, o2, o3, gcat_ref, part_a, part_b, sums_ref, gain_vm, shift_vm, out_vm, acc_vm,
):
    me = me_ref[0]
    rows, width = v_ref.shape
    size = rows // 4
    for c in range(4):
        @pl.when(me == c)
        def _(c=c):
            at = slice((c % 2) * width, (c % 2 + 1) * width)
            gain_vm[...] = vec_ref[c // 2 : c // 2 + 1, at]
            shift_vm[...] = vec_ref[c // 2 + 2 : c // 2 + 3, at]
    mine, other = mine_ref[...], other_ref[...]
    mean_m, mean_o = mine[:, 0:1], other[:, 0:1]
    mean = 0.5 * (mean_m + mean_o)
    gap = mean_m - mean_o
    spread = mine[:, 1:2] + other[:, 1:2] + (0.5 * width) * gap * gap
    inverse = 0.5 / width
    r = lax.rsqrt(spread * inverse + epsilon)
    mean_cg = (mine[:, 2:3] + other[:, 2:3]) * inverse
    cross = (
        mine[:, 3:4] + (mean_m - mean) * mine[:, 2:3] + other[:, 3:4] + (mean_o - mean) * other[:, 2:3]
    )
    mean_cgx = cross * inverse * r
    gain = gain_vm[...]
    cot = cot_ref[...].astype(F32)
    xhat = (v_ref[...] - mean) * r
    out_vm[...] = (xhat * gain + shift_vm[...]).astype(BF16)
    for k, out in enumerate((o0, o1, o2, o3)):
        out[...] = out_vm[rows_at(me, k, size), :]
    g = r * (cot * gain - mean_cg - xhat * mean_cgx)
    g_low = g.astype(BF16)
    g_wide = g_low.astype(F32)
    row_i = lax.broadcasted_iota(jnp.int32, (rows, width), 0)
    after = jnp.where(row_i == rows - 1, 0.0, pltpu.roll(g_wide, rows - 1, 0)).astype(BF16)
    before = jnp.where(row_i == 0, 0.0, pltpu.roll(g_wide, 1, 0)).astype(BF16)
    gcat_ref[0] = after
    gcat_ref[1] = g_low
    gcat_ref[2] = before
    sums_ref[...] = jnp.zeros(sums_ref.shape, F32)
    sums_ref[0:1, :] = jnp.sum(cot * xhat, axis=0, keepdims=True)
    sums_ref[1:2, :] = jnp.sum(cot, axis=0, keepdims=True)
    sums_ref[2:3, :] = jnp.sum(g_wide, axis=0, keepdims=True)
    acc_vm[...] = dot_nt(after, w_ref[0]) + dot_nt(g_low, w_ref[1]) + dot_nt(before, w_ref[2])
    for c in range(4):
        @pl.when(me == c)
        def _(c=c):
            acc_vm[:, c * width : (c + 1) * width] += g
    for k, (out, off) in enumerate(((part_b, 0), (part_b, size), (part_a, 0), (part_a, size))):
        out[off : off + size, :] = acc_vm[rows_at(me, k, size), :].astype(BF16)


def merge_backward(me, v, cot, mine, other, w, vecs):
    rows, width = v.shape
    outs = (
        [((rows // 4, width), BF16)] * 4
        + [((3, rows, width), BF16)]
        + [((rows // 2, 2 * D), BF16)] * 2
        + [((8, width), F32)]
    )
    scratch = [((1, width), F32)] * 2 + [((rows, width), BF16), ((rows, 2 * D), F32)]
    return full_call(
        merge_backward_kernel, outs, scratch, 6 * rows * 2 * D * width,
        me, v, cot, mine, other, w, vecs,
    )


def merge_weight_kernel(joined_ref, gcat_ref, *outs):
    joined_t = joined_ref[...].T
    for o, out_ref in enumerate(outs):
        out_ref[...] = dot_nn(joined_t, gcat_ref[o]).astype(BF16)


def merge_weight_grad(joined, gcat):
    rows, width = gcat.shape[1:]
    outs = [((joined.shape[1], width), BF16)] * 3
    return full_call(
        merge_weight_kernel, outs, [], 6 * rows * joined.shape[1] * width, joined, gcat
    )


def layer_norm(values, gain_vec, shift_vec):
    row_mean = jnp.mean(values, axis=-1, keepdims=True)
    centered = values - row_mean
    row_var = jnp.mean(centered * centered, axis=-1, keepdims=True)
    return centered * lax.rsqrt(row_var + epsilon) * gain_vec + shift_vec


def gelu_exact(values):
    return jax.nn.gelu(values, approximate=False)


def rounded(values):
    return values.astype(jnp.bfloat16)


def wide(values):
    return values.astype(jnp.float32)


def pad_units(array, axis):
    pads = [(0, 0)] * array.ndim
    pads[axis] = (0, LANES - array.shape[axis])
    return jnp.pad(array, pads)


def swap(array, axis, bit, size):
    return lax.ppermute(array, axis, [(i, i ^ bit) for i in range(size)])


def across(array, bit):
    return swap(array, "tensor", bit, 4)


def gather(own):
    far = across(own, 2)
    near = across(own, 1)
    return [own, far, near, across(far, 1)]


def scatter(part_a, part_b):
    size = part_b.shape[0] // 2
    near = across(part_a, 1)
    passed = rounded(wide(part_b[size:]) + wide(near[size:]))
    far = across(passed, 2)
    return wide(part_b[:size]) + wide(near[:size]) + wide(far)


def halves(part):
    low = rounded(part)
    count = low.shape[0] // 2
    return low[count:], low[:count]


def make_body(dp_size):
    def total_small(values):
        bit = 1
        while bit < dp_size:
            values = values + swap(values, "dp", bit, dp_size)
            bit *= 2
        return values

    all_bits = [1 << k for k in range(dp_size.bit_length() - 1)]

    class Total:
        def __init__(self, part, first):
            self.bits = all_bits[first:] + all_bits[:first]
            self.level = 0
            self.rising = False
            self.result = None
            self.send_half(rounded(part))

        def upper(self):
            return (lax.axis_index("dp") & self.bits[self.level]) != 0

        def swap(self, part):
            return swap(part, "dp", self.bits[self.level], dp_size)

        def send_half(self, part):
            if self.level == len(self.bits) - 1:
                self.keep, self.got = part, self.swap(part)
                return
            half = part.shape[0] // 2
            low, high = part[:half], part[half:]
            self.keep = jnp.where(self.upper(), high, low)
            self.got = self.swap(jnp.where(self.upper(), low, high))

        def step(self):
            if self.result is not None:
                return
            if self.rising:
                low = jnp.where(self.upper(), self.got, self.keep)
                high = jnp.where(self.upper(), self.keep, self.got)
                own = jnp.concatenate([low, high])
            else:
                own = rounded(wide(self.keep) + wide(self.got))
                if self.level < len(self.bits) - 1:
                    self.level += 1
                    self.send_half(own)
                    return
                self.rising = True
            self.level -= 1
            if self.level < 0:
                self.result = own
            else:
                self.keep, self.got = own, self.swap(own)

    def finish(parts):
        while any(part.result is None for part in parts):
            for part in parts:
                part.step()

    def slot(values, parts):
        values, gots = lax.optimization_barrier((values, [part.got for part in parts]))
        for part, got in zip(parts, gots):
            part.got = got
            part.step()
        return values

    def body(
        tokens,
        chars,
        lengths,
        mask,
        qkv_weight,
        qkv_bias,
        out_weight,
        out_bias,
        attn_gain,
        attn_shift,
        ffn_in_weight,
        ffn_in_bias,
        ffn_out_weight,
        ffn_out_bias,
        ffn_gain,
        ffn_shift,
        gru_weight,
        gate_bias,
        cand_bias,
        char_weight,
        char_bias,
        merge_weight,
        merge_bias,
        token_gain,
        token_shift,
        char_gain,
        char_shift,
        token_cot,
        char_cot,
    ):
        place = lax.axis_index("tensor")
        me = place.astype(jnp.int32).reshape(1)
        head_count = qkv_weight.shape[2]
        unit_count = gru_weight.shape[3]
        tok_all = jnp.concatenate(gather(tokens))
        chr_blocks = gather(chars)
        seq_rows = tok_all.shape[0]
        cot_parts = column_blocks(me, token_cot, char_cot)
        cot_blocks = [cot_parts[0]] + [across(cot_parts[k], ORDER[k]) for k in range(1, 4)]
        projected = jnp.dot(
            tok_all, qkv_weight.reshape(D, -1), preferred_element_type=jnp.float32
        ).reshape(seq_rows, 3, head_count, HD)
        queries = rounded((projected[:, 0] + qkv_bias[0]) * 0.125)
        key_rows = rounded(projected[:, 1])
        values = rounded(projected[:, 2] + qkv_bias[1])
        scores = jnp.einsum("qhd,khd->hqk", queries, key_rows, preferred_element_type=jnp.float32)
        maxima = jnp.max(scores, axis=-1, keepdims=True)
        totals = jnp.sum(jnp.exp(scores - maxima), axis=-1, keepdims=True)
        log_norm = maxima + jnp.log(totals)
        probs_low = rounded(jnp.exp(scores - log_norm))
        mixed = rounded(
            jnp.einsum("hqk,khd->qhd", probs_low, values, preferred_element_type=jnp.float32)
        ).reshape(seq_rows, head_count * HD)
        attn_part = jnp.dot(mixed, out_weight.reshape(-1, D), preferred_element_type=jnp.float32)
        wide_gru = pad_units(gru_weight, 3).reshape(CE, -1)
        wide_bias = pad_units(jnp.stack([gate_bias, cand_bias]), 2).reshape(1, -1)
        wide_char = pad_units(char_weight, 1).reshape(-1, D)
        update, excess, pooled_low, char_a, char_b = gru_forward(
            me, chr_blocks, wide_gru, wide_bias, lengths, mask, wide_char
        )
        attn_rows = scatter(*halves(attn_part))
        vecs = jnp.stack([token_gain, char_gain, token_shift, char_shift])
        wide_merge_bias = merge_bias.reshape(1, -1)
        attn_rows, cot_blocks, vecs, wide_merge_bias = lax.optimization_barrier(
            (attn_rows, cot_blocks, vecs, wide_merge_bias)
        )
        first_in = wide(tokens) + attn_rows + out_bias
        first_out, first_pull = jax.vjp(layer_norm, first_in, attn_gain, attn_shift)
        first_low_all = jnp.concatenate(gather(rounded(first_out)))
        hidden_pre = (
            jnp.dot(first_low_all, ffn_in_weight, preferred_element_type=jnp.float32) + ffn_in_bias
        )
        inter_low = rounded(gelu_exact(hidden_pre))
        ffn_part = jnp.dot(inter_low, ffn_out_weight, preferred_element_type=jnp.float32)
        char_mid = scatter(char_a, char_b) + char_bias
        mid_blocks = gather(rounded(char_mid))
        ffn_sum = scatter(*halves(ffn_part))
        second_out, second_pull = jax.vjp(
            layer_norm, first_out + ffn_sum + ffn_out_bias, ffn_gain, ffn_shift
        )
        second_blocks = gather(rounded(second_out))
        joined, mixed_cols, cot_cols, stats = merge_forward(
            me, second_blocks, mid_blocks, cot_blocks, merge_weight, wide_merge_bias, vecs,
        )
        other_stats = across(stats, 1)
        *out_parts, g_cat, joint_a, joint_b, merge_sums = merge_backward(
            me, mixed_cols, cot_cols, stats, other_stats, merge_weight, vecs
        )
        out_blocks = [out_parts[0]] + [across(out_parts[k], ORDER[k]) for k in range(1, 4)]
        token_out, char_out = from_columns(me, out_blocks)
        g_rows = scatter(joint_a, joint_b)
        merge_a, merge_b, merge_c = [
            Total(part, first) for part, first in zip(merge_weight_grad(joined, g_cat), (0, 0, 1))
        ]
        g_mid_low = rounded(g_rows[:, D:])
        ffn_in_grad, grad_ffn_gain, grad_ffn_shift = second_pull(g_rows[:, :D])
        ffn_grad_low = rounded(ffn_in_grad)
        grad_ffn_out_bias = jnp.sum(wide(ffn_grad_low), axis=0)
        grad_char_bias = jnp.sum(wide(g_mid_low), axis=0)
        ffn_grad_all = jnp.concatenate(gather(ffn_grad_low))
        g_mid_blocks = gather(g_mid_low)
        hidden_again, ffn_grad_all = lax.optimization_barrier((hidden_pre, ffn_grad_all))
        inter_grad = jnp.einsum(
            "td,fd->tf", ffn_grad_all, ffn_out_weight, preferred_element_type=jnp.float32
        )
        hidden_grad = rounded(jax.vjp(gelu_exact, hidden_again)[1](inter_grad)[0])
        first_part = jnp.einsum(
            "tf,cf->tc", hidden_grad, ffn_in_weight, preferred_element_type=jnp.float32
        )
        grad_ffn_in_bias = jnp.sum(wide(hidden_grad), axis=0)
        grad_ffn_in_weight = jnp.einsum(
            "tc,tf->cf", first_low_all, hidden_grad, preferred_element_type=jnp.float32
        )
        grad_ffn_out_weight = jnp.einsum(
            "tf,td->fd", inter_low, ffn_grad_all, preferred_element_type=jnp.float32
        )
        first_part, grad_ffn_in_weight, grad_ffn_out_weight = slot(
            (rounded(first_part), rounded(grad_ffn_in_weight), rounded(grad_ffn_out_weight)),
            [merge_a, merge_c],
        )
        ffn_out_total = Total(grad_ffn_out_weight, 0)
        ffn_in_total = Total(grad_ffn_in_weight, 0)
        first_rows = scatter(*halves(first_part))
        g_chr_a, g_chr_b, wide_gru_grad, wide_bias_grad, wide_char_grad = gru_backward(
            me, g_mid_blocks, wide_char, pooled_low, update, excess, chr_blocks, wide_gru,
            lengths, mask,
        )
        chars_grad = rounded(scatter(g_chr_a, g_chr_b))
        wide_bias_grad = wide_bias_grad.reshape(2, 2, LANES)[..., :unit_count]
        first_rows = slot(first_rows, [merge_b])
        g_resid, grad_attn_gain, grad_attn_shift = first_pull(ffn_in_grad + first_rows)
        g_attn_low = rounded(g_resid)
        grad_out_bias = jnp.sum(wide(g_attn_low), axis=0)
        g_attn_blocks, wide_gru_grad, wide_char_grad = slot(
            (gather(g_attn_low), wide_gru_grad, wide_char_grad), [merge_a, merge_c]
        )
        grad_gru_weight = wide_gru_grad.reshape(CE, 2, 2, LANES)[..., :unit_count]
        grad_char_weight = wide_char_grad.reshape(2, LANES, D)[:, :unit_count]
        char_rows = grad_char_weight.size // D
        units_total = Total(
            jnp.concatenate([grad_char_weight.reshape(-1, D), grad_gru_weight.reshape(-1, D)]), 1
        )
        g_attn_all = jnp.concatenate(g_attn_blocks)
        grad_out_weight = jnp.einsum(
            "tk,td->kd", mixed, g_attn_all, preferred_element_type=jnp.float32
        ).reshape(out_weight.shape)
        g_mixed = rounded(
            jnp.einsum(
                "td,kd->tk", g_attn_all, out_weight.reshape(-1, D),
                preferred_element_type=jnp.float32,
            )
        ).reshape(seq_rows, head_count, HD)
        scores_again = jnp.einsum(
            "qhd,khd->hqk", queries, key_rows, preferred_element_type=jnp.float32
        )
        probs_again = jnp.exp(scores_again - log_norm)
        probs_again_low = rounded(probs_again)
        g_values = jnp.einsum(
            "hqk,qhd->khd", probs_again_low, g_mixed, preferred_element_type=jnp.float32
        )
        g_probs = jnp.einsum("qhd,khd->hqk", g_mixed, values, preferred_element_type=jnp.float32)
        g_scores = rounded(
            probs_again * (g_probs - jnp.sum(g_probs * probs_again, axis=-1, keepdims=True))
        )
        g_queries = jnp.einsum(
            "hqk,khd->qhd", g_scores, key_rows, preferred_element_type=jnp.float32
        )
        g_keys = jnp.einsum("hqk,qhd->khd", g_scores, queries, preferred_element_type=jnp.float32)
        g_project = jnp.stack(
            [rounded(g_queries) * 0.125, rounded(g_keys), rounded(g_values)], axis=1
        )
        g_flat = slot(g_project.reshape(seq_rows, -1), [merge_b, ffn_out_total])
        grad_qkv_weight = jnp.einsum(
            "tc,tf->cf", tok_all, g_flat, preferred_element_type=jnp.float32
        ).reshape(qkv_weight.shape)
        grad_qkv_bias = jnp.stack(
            [jnp.sum(wide(g_project[:, 0]), axis=0), jnp.sum(wide(g_project[:, 2]), axis=0)]
        )
        g_tok_all = jnp.einsum(
            "tf,cf->tc", g_flat, qkv_weight.reshape(D, -1), preferred_element_type=jnp.float32
        )
        width = qkv_weight.shape[1] * head_count * HD
        heads = jnp.concatenate(
            [
                rounded(grad_qkv_weight).reshape(D, width),
                rounded(grad_out_weight).reshape(-1, width),
            ]
        )
        g_tok_all, heads = slot(
            (rounded(g_tok_all), heads), [merge_a, merge_c, ffn_in_total]
        )
        half = heads.shape[0] // 2
        heads_a, heads_b = Total(heads[:half], 0), Total(heads[half:], 1)
        token_grad = rounded(g_resid + scatter(*halves(g_tok_all)))
        width = merge_sums.shape[1]
        col_grads = lax.dynamic_update_slice(
            jnp.zeros((2, 4 * width), jnp.float32), merge_sums[0:2], (0, place * width)
        ).reshape(4, D)
        row_grads = jnp.stack(
            [
                grad_out_bias,
                grad_attn_gain,
                grad_attn_shift,
                grad_ffn_out_bias,
                grad_ffn_gain,
                grad_ffn_shift,
                grad_char_bias,
            ]
        )
        norm_parts = jnp.concatenate([row_grads, col_grads])
        norm_parts = norm_parts + across(norm_parts, 1)
        norm_parts = norm_parts + across(norm_parts, 2)
        norm_rows = lax.dynamic_slice_in_dim(norm_parts, place * (D // 4), D // 4, 1)
        smalls = [
            norm_rows,
            wide_bias_grad,
            merge_sums[2],
            grad_ffn_in_bias,
            grad_qkv_bias,
        ]
        flat = jnp.concatenate([small.reshape(-1) for small in smalls])
        flat = total_small(flat)
        totals = []
        start = 0
        for small in smalls:
            totals.append(flat[start : start + small.size].reshape(small.shape))
            start += small.size
        norm_rows, gate_grads, grad_merge_bias, grad_ffn_in_bias, grad_qkv_bias = totals
        finish(
            [merge_b, merge_a, merge_c, ffn_out_total, ffn_in_total, units_total, heads_a, heads_b]
        )
        grad_merge_weight = wide(jnp.stack([merge_a.result, merge_b.result, merge_c.result]))
        grad_ffn_out_weight = wide(ffn_out_total.result)
        grad_ffn_in_weight = wide(ffn_in_total.result)
        units = wide(units_total.result)
        grad_char_weight = units[:char_rows].reshape(grad_char_weight.shape)
        grad_gru_weight = units[char_rows:].reshape(grad_gru_weight.shape)
        heads = jnp.concatenate([heads_a.result, heads_b.result])
        grad_qkv_weight = wide(heads[:D]).reshape(grad_qkv_weight.shape)
        grad_out_weight = wide(heads[D:].reshape(grad_out_weight.shape))
        return (
            token_out,
            char_out,
            token_grad,
            chars_grad,
            grad_qkv_weight,
            grad_qkv_bias,
            grad_out_weight,
            norm_rows[0],
            norm_rows[1],
            norm_rows[2],
            grad_ffn_in_weight,
            grad_ffn_in_bias,
            grad_ffn_out_weight,
            norm_rows[3],
            norm_rows[4],
            norm_rows[5],
            grad_gru_weight,
            gate_grads[0],
            gate_grads[1],
            grad_char_weight,
            norm_rows[6],
            grad_merge_weight,
            grad_merge_bias,
            norm_rows[7],
            norm_rows[9],
            norm_rows[8],
            norm_rows[10],
        )

    return body


def solution(mesh):
    in_specs = (
        P(("dp", "tensor"), None),
        P(("dp", "tensor"), None),
        P("dp", None),
        P("dp", None),
        P(None, None, "tensor", None),
        P(None, "tensor", None),
        P("tensor", None, None),
        P(),
        P(),
        P(),
        P(None, "tensor"),
        P("tensor"),
        P("tensor", None),
        P(),
        P(),
        P(),
        P(None, None, None, "tensor"),
        P(None, "tensor"),
        P(None, "tensor"),
        P(None, "tensor", None),
        P(),
        P(None, None, "tensor"),
        P("tensor"),
        P(),
        P(),
        P(),
        P(),
        P(("dp", "tensor"), None),
        P(("dp", "tensor"), None),
    )
    out_specs = (
        P(("dp", "tensor"), None),
        P(("dp", "tensor"), None),
        P(("dp", "tensor"), None),
        P(("dp", "tensor"), None),
        P(None, None, "tensor", None),
        P(None, "tensor", None),
        P("tensor", None, None),
        P("tensor"),
        P("tensor"),
        P("tensor"),
        P(None, "tensor"),
        P("tensor"),
        P("tensor", None),
        P("tensor"),
        P("tensor"),
        P("tensor"),
        P(None, None, None, "tensor"),
        P(None, "tensor"),
        P(None, "tensor"),
        P(None, "tensor", None),
        P("tensor"),
        P(None, None, "tensor"),
        P("tensor"),
        P("tensor"),
        P("tensor"),
        P("tensor"),
        P("tensor"),
    )
    return jax.shard_map(
        make_body(mesh.shape["dp"]), mesh=mesh, in_specs=in_specs, out_specs=out_specs, check_vma=False)
```
